32 devices in a mesh: batch: 4 (over y, x), heads: 8 (over z, core).
Axes of the slice: x: 2, y: 2, z: 4, core: 2. Of those that a mesh axis runs over, the one named last changes fastest.
Arguments:
- tokens: bfloat16 [2, 1024, 4, 2048], P(None, 'heads', 'batch'), may hold values from -6 to 6
- out_grad: bfloat16 [2, 1024, 4, 2048], P(None, 'heads', 'batch'), may hold values from -6 to 6
- row_seq: int32 [2, 4], P(None, 'batch'), may hold values from 0 to 7, as said below
- seq_lengths: int32 [8], replicated, may hold values from 384 to 1024, as said below
- norm1_gain: float32 [2048], P(('batch', 'heads')), may hold values from 0.5 to 1.5
- norm1_bias: float32 [2048], P(('batch', 'heads')), may hold values from -1.25 to 1.25
- qkv_weight: bfloat16 [2048, 3, 2048], P(None, None, 'heads'), may hold values from -0.125 to 0.125
- qk_bias: bfloat16 [2, 32, 64], P(None, 'heads'), may hold values from -3 to 3
- v_bias: bfloat16 [32, 64], P('heads'), may hold values from -0.25 to 0.25
- out_weight: bfloat16 [2048, 2048], P('heads'), may hold values from -0.75 to 0.75
- norm2_gain: float32 [2048], P(('batch', 'heads')), may hold values from 0.5 to 1.5
- norm2_bias: float32 [2048], P(('batch', 'heads')), may hold values from -1.25 to 1.25
- gate_weight: bfloat16 [2048, 5632], P('batch', 'heads'), may hold values from -0.125 to 0.125
- up_weight: bfloat16 [2048, 5632], P('batch', 'heads'), may hold values from -0.125 to 0.125
- down_weight: bfloat16 [2048, 5632], P('batch', 'heads'), may hold values from -0.078125 to 0.078125
Outputs:
- layer_out: bfloat16 [2, 1024, 4, 2048], P(None, 'heads', 'batch')
- input_grad: bfloat16 [2, 1024, 4, 2048], P(None, 'heads', 'batch')
- norm1_gain_grad: float32 [2048], P(('batch', 'heads'))
- norm1_bias_grad: float32 [2048], P(('batch', 'heads'))
- qkv_weight_grad: float32 [2048, 3, 2048], P('batch', None, 'heads')
- qk_bias_grad: float32 [2, 32, 64], P(None, 'heads', 'batch')
- v_bias_grad: float32 [32, 64], P('heads', 'batch')
- out_weight_grad: float32 [2048, 2048], P('heads', 'batch')
- norm2_gain_grad: float32 [2048], P(('batch', 'heads'))
- norm2_bias_grad: float32 [2048], P(('batch', 'heads'))
- gate_weight_grad: float32 [2048, 5632], P('batch', 'heads')
- up_weight_grad: float32 [2048, 5632], P('batch', 'heads')
- down_weight_grad: float32 [2048, 5632], P('batch', 'heads')
The draws below stay inside these ranges and needn't reach their ends.
Inputs may be any that keep to these rules, and one draw needn't show every extreme that they name: `seq_lengths`: each index of batch holds 2 rows over all micro-batches; one of them holds a sequence of exactly 1024 tokens. `row_seq`: every sequence number is held by exactly one row.
All inputs are finite; a program needn't handle non-finite values.
Results may differ from the reference program's by a relative error of at most 0.024.
Values may be sent and summed in bfloat16 or wider, within the bound.
No kernel may reach another device: no remote copies, remote signals or barrier semaphores. Data moves between devices by JAX's collectives and lax.ppermute only.
A program may use at most 192 MiB of HBM per device.

```python
from functools import partial
import jax
import jax.numpy as jnp
from jax import lax

D = 2048
HEADS = 32
HD = 64
ROT = 16
FF = 5632
SEQ = 1024
LEN_MIN = 384
MB = 2
ROWS_DEV = 1
ROWS = 4


def joint_rows(key):
    base = jax.random.fold_in(key, 7)
    first_key, second_key, third_key = jax.random.split(base, 3)
    group_size = MB * ROWS_DEV
    raw_draws = jax.random.randint(first_key, (MB, ROWS), 0, 1024)
    tail_part = raw_draws * raw_draws // 1024 * raw_draws // 1024
    lengths = LEN_MIN + tail_part * (SEQ - LEN_MIN) // 1023
    batch_pos = jnp.arange(MB, dtype=jnp.int32)[:, None]
    row_pos = jnp.arange(ROWS, dtype=jnp.int32)[None, :]
    member = batch_pos * ROWS_DEV + row_pos % ROWS_DEV
    owner_index = row_pos // ROWS_DEV
    chosen = jax.random.randint(second_key, (ROWS // ROWS_DEV,), 0, group_size)
    chosen_here = chosen[owner_index]
    lengths = jnp.where(member == chosen_here, SEQ, lengths)
    shortest = (owner_index == 0) & (member == (chosen[0] + 1) % group_size)
    lengths = jnp.where(shortest, LEN_MIN, lengths)
    row_order = jax.random.permutation(third_key, MB * ROWS).astype(jnp.int32)
    inverse = jnp.argsort(row_order, stable=True)
    seq_len_all = lengths.reshape(MB * ROWS)[inverse]
    return (row_order.reshape(MB, ROWS), seq_len_all.astype(jnp.int32))


def draw_row_seq(key, part):
    return joint_rows(key)[0]


def draw_seq_lengths(key, part):
    return joint_rows(key)[1]


def block_scale(stream_key, shape, shards, low, largest):
    gain, own = 1.0, jax.random.fold_in(stream_key, 6)
    for dim, parts in shards:
        draws = jnp.exp(jax.random.uniform(jax.random.fold_in(own, dim), (parts,), jnp.float32, low / len(shards), largest / len(shards)))
        gain = gain * jnp.repeat(draws, shape[dim] // parts).reshape([-1 if axis == dim else 1 for axis in range(len(shape))])
    return gain


def gaussian(stream_key, extent, scale, reach, cuts=(), kind=jnp.bfloat16):
    factor_of = block_scale(stream_key, extent, cuts, -0.22, 0.18) if cuts else 1.0
    entries = jax.random.normal(stream_key, extent, jnp.float32) * scale * factor_of
    return jnp.minimum(jnp.maximum(entries, -reach), reach).astype(kind)


def setup_inputs(seed: int = 0) -> dict:
    key_list = jax.random.split(jax.random.key(seed), 16)
    return {
        "tokens": gaussian(key_list[0], (MB, SEQ, ROWS, D), 1.0, 6.0, ((1, 8), (2, 4))),
        "out_grad": gaussian(key_list[1], (MB, SEQ, ROWS, D), 1.0, 6.0, ((1, 8), (2, 4))),
        "row_seq": draw_row_seq(jax.random.fold_in(key_list[15], 71), 0),
        "seq_lengths": draw_seq_lengths(jax.random.fold_in(key_list[15], 71), 0),
        "norm1_gain": jnp.clip(1.0 + 0.1 * jax.random.normal(key_list[4], (D,), jnp.float32), 0.5, 1.5),
        "norm1_bias": gaussian(key_list[5], (D,), 0.2, 1.25, ((0, 32),), jnp.float32),
        "qkv_weight": gaussian(key_list[6], (D, 3, HEADS * HD), D ** -0.5, 0.125, ((2, 8),)),
        "qk_bias": gaussian(key_list[7], (2, HEADS, HD), 0.5, 3.0, ((1, 8),)),
        "v_bias": gaussian(key_list[8], (HEADS, HD), 0.04, 0.25, ((0, 8),)),
        "out_weight": gaussian(key_list[9], (HEADS * HD, D), (HEADS * HD // 32) ** -0.5, 0.75, ((0, 8),)),
        "norm2_gain": jnp.clip(1.0 + 0.1 * jax.random.normal(key_list[10], (D,), jnp.float32), 0.5, 1.5),
        "norm2_bias": gaussian(key_list[11], (D,), 0.2, 1.25, ((0, 32),), jnp.float32),
        "gate_weight": gaussian(key_list[12], (D, FF), D ** -0.5, 0.125, ((0, 4), (1, 8))),
        "up_weight": gaussian(key_list[13], (D, FF), D ** -0.5, 0.125, ((0, 4), (1, 8))),
        "down_weight": gaussian(key_list[14], (D, FF), FF ** -0.5, 0.078125, ((0, 4), (1, 8))),
    }


eps = 1e-05
neg_big = -1e+30
rope_base = 10000.0
highest = lax.Precision.HIGHEST

@jax.custom_vjp
def low(v):
    return lax.optimization_barrier(v.astype(jnp.bfloat16)).astype(jnp.float32)

@jax.custom_vjp
def low_back(v):
    return v

def low_keep(v):
    return (low(v), None)

def low_pass(kept, grad):
    return (grad,)

def back_keep(v):
    return (v, None)

def back_low(kept, grad):
    return (low(grad),)
low.defvjp(low_keep, low_pass)
low_back.defvjp(back_keep, back_low)

def layer_norm(values, gain_vec, shift_vec):
    average = lax.optimization_barrier(jnp.mean(values, axis=-1, keepdims=True))
    centred = values - average
    inverse = lax.rsqrt(lax.optimization_barrier(jnp.mean(centred * centred, axis=-1, keepdims=True)) + eps)
    return centred * inverse * gain_vec + shift_vec

def rope_tables(length_all):
    half_rot = ROT // 2
    frequency = rope_base ** (-(2.0 * jnp.arange(half_rot, dtype=jnp.float32)) / ROT)
    angles = jnp.arange(length_all, dtype=jnp.float32)[:, None] * frequency[None, :]
    return (jnp.cos(angles), jnp.sin(angles))

def rotate(values, cosine, sine):
    half_rot = ROT // 2
    first_half = values[..., :half_rot]
    second_half = values[..., half_rot:ROT]
    return jnp.concatenate([first_half * cosine - second_half * sine, second_half * cosine + first_half * sine, values[..., ROT:]], axis=-1)

def head_attention(visible, query, keys, values):
    scores = low_back(jnp.dot(query, keys.T, precision=highest) * HD ** (-0.5))
    scores = jnp.where(visible, scores, neg_big)
    row_top = lax.optimization_barrier(jnp.max(scores, axis=-1, keepdims=True))
    weights = jnp.exp(scores - row_top)
    normalized = weights / lax.optimization_barrier(jnp.sum(weights, axis=-1, keepdims=True))
    return jnp.dot(low(normalized), values, precision=highest)

def layer_row(params, row_item):
    x_row, length = row_item
    gain_one, shift_one, qkv_w, qk_b, v_b, out_w, gain_two, shift_two, gate_w, up_w, down_w = params
    positions = jnp.arange(SEQ, dtype=jnp.int32)
    visible = (positions[None, :] <= positions[:, None]) & (positions[None, :] < length)
    cosine, sine = rope_tables(SEQ)
    cosine = cosine[:, None, :]
    sine = sine[:, None, :]
    width_all = HEADS * HD
    normed_one = low(layer_norm(x_row, gain_one, shift_one))
    projected = jnp.einsum('sd,dcj->scj', normed_one, qkv_w, precision=highest)
    query = low(rotate(low_back(projected[:, 0] + qk_b[0].reshape(width_all)).reshape(SEQ, HEADS, HD), cosine, sine))
    keys = low(rotate(low_back(projected[:, 1] + qk_b[1].reshape(width_all)).reshape(SEQ, HEADS, HD), cosine, sine))
    values = low(low_back(projected[:, 2] + v_b.reshape(width_all))).reshape(SEQ, HEADS, HD)
    attend = jax.checkpoint(partial(head_attention, visible))

    def one_head(head_item):
        return attend(head_item[0], head_item[1], head_item[2])
    mixed = lax.map(one_head, (query.transpose(1, 0, 2), keys.transpose(1, 0, 2), values.transpose(1, 0, 2)))
    mixed = low(low_back(mixed.transpose(1, 0, 2).reshape(SEQ, width_all)))
    branch = low_back(jnp.dot(mixed, out_w, precision=highest))
    state = x_row + branch
    normed_two = low(layer_norm(state, gain_two, shift_two))
    gate_value = low_back(jnp.dot(normed_two, gate_w, precision=highest))
    up_value = low_back(jnp.dot(normed_two, up_w, precision=highest))
    inner = low(jax.nn.silu(gate_value) * up_value)
    mlp_result = low_back(jnp.dot(inner, down_w.T, precision=highest))
    valid = (positions < length).astype(jnp.float32)
    return (state + mlp_result) * valid[:, None]

def forward(params, inputs, row_len):
    rows_all = inputs.transpose(0, 2, 1, 3).reshape(MB * ROWS, SEQ, D)
    layer = jax.checkpoint(partial(layer_row, params))
    result = lax.map(layer, (rows_all, row_len.reshape(MB * ROWS)))
    return result.reshape(MB, ROWS, SEQ, D).transpose(0, 2, 1, 3)

def reference(tokens, out_grad, row_seq, seq_lengths, norm1_gain, norm1_bias, qkv_weight, qk_bias, v_bias, out_weight, norm2_gain, norm2_bias, gate_weight, up_weight, down_weight):
    table = jnp.arange(MB * ROWS, dtype=jnp.int32)
    row_len = lax.optimization_barrier(jnp.sum(jnp.where(row_seq[..., None] == table, seq_lengths, 0), axis=-1)).astype(jnp.int32)
    params = (norm1_gain.astype(jnp.float32), norm1_bias.astype(jnp.float32), qkv_weight.astype(jnp.float32), qk_bias.astype(jnp.float32), v_bias.astype(jnp.float32), out_weight.astype(jnp.float32), norm2_gain.astype(jnp.float32), norm2_bias.astype(jnp.float32), gate_weight.astype(jnp.float32), up_weight.astype(jnp.float32), down_weight.astype(jnp.float32))

    def wrapped(inputs, weights_all):
        return forward(weights_all, inputs, row_len)
    result, pullback = jax.vjp(wrapped, tokens.astype(jnp.float32), params)
    grad_in, grads = pullback(out_grad.astype(jnp.float32))
    return (result.astype(jnp.bfloat16), grad_in.astype(jnp.bfloat16), grads[0], grads[1], grads[2], grads[3], grads[4], grads[5], grads[6], grads[7], grads[8], grads[9], grads[10])
```

```python
import functools
import math

import jax
import jax.numpy as jnp
from jax import lax
from jax.experimental import pallas as pl
from jax.experimental.pallas import tpu as pltpu
from jax.sharding import PartitionSpec as P

HD = 64
ROT = 16
EPS = 1e-05
NEG = -1e30
ROPE_BASE = 10000.0
SCALE = HD ** (-0.5)
LOG2E = math.log2(math.e)
F32 = jnp.float32
BF16 = jnp.bfloat16


def dot(a, b, ca, cb):
    return lax.dot_general(a, b, (((ca,), (cb,)), ((), ())), preferred_element_type=F32)


def row_norm(values, gain_vec, shift_vec):
    average = jnp.mean(values, axis=-1, keepdims=True)
    centred = values - average
    inverse = lax.rsqrt(jnp.mean(centred * centred, axis=-1, keepdims=True) + EPS)
    unit_rows = centred * inverse
    return (unit_rows * gain_vec + shift_vec, unit_rows, inverse)


def norm_back(gradient, unit_rows, inverse, gain_vec):
    scaled_grad = gradient * gain_vec
    return inverse * (
        scaled_grad
        - jnp.mean(scaled_grad, axis=-1, keepdims=True)
        - unit_rows * jnp.mean(scaled_grad * unit_rows, axis=-1, keepdims=True)
    )


class Line:
    def __init__(self):
        self.devices = lax.axis_size("heads")
        self.chips = self.devices // 2
        index = lax.axis_index("heads")
        self.chip = index // 2
        self.core = index % 2

    def hop(self, value, sources, step):
        pairs = [(2 * i + c, 2 * (i + step) + c) for i in sources for c in range(2)]
        return lax.ppermute(value, "heads", pairs)

    def swap(self, value):
        pairs = [(2 * i + c, 2 * i + 1 - c) for i in range(self.chips) for c in range(2)]
        return lax.ppermute(value, "heads", pairs)

    def gather(self, block):
        n = self.chips
        ups, downs = [block], [block]
        for step in range(1, n):
            ups.append(self.hop(ups[-1], range(step - 1, n - 1), 1))
            downs.append(self.hop(downs[-1], range(1, n - step + 1), -1))
        pieces = [block]
        for k in range(1, n):
            pieces.append(jnp.where(self.chip >= k, ups[k], downs[n - k]))
        return jnp.concatenate(pieces, axis=0)

    def scatter(self, pieces):
        n = self.chips
        up = down = None
        for m in range(n - 1, 0, -1):
            value_up = pieces[n - m] if up is None else add_low(pieces[n - m], up)
            value_down = pieces[m] if down is None else add_low(pieces[m], down)
            up = self.hop(value_up, range(0, n - m), 1)
            down = self.hop(value_down, range(m, n), -1)
        return pieces[0].astype(F32) + up.astype(F32) + down.astype(F32)


def after(value, *earlier):
    return lax.optimization_barrier((value, *earlier))[0]


def add_low(a, b):
    return (a.astype(F32) + b.astype(F32)).astype(BF16)


def shifts(value_of, axis):
    n = lax.axis_size(axis)
    received = [value_of(0)]
    for k in range(1, n):
        received.append(lax.ppermute(value_of(k), axis, [(i, (i + k) % n) for i in range(n)]))
    return received


def small_gather(value, axis):
    n = lax.axis_size(axis)
    received = shifts(lambda k: value, axis)
    width = value.shape[1]
    ordered = jnp.concatenate(received[::-1], axis=1)
    doubled = jnp.concatenate([ordered, ordered], axis=1)
    start = (n - 1 - lax.axis_index(axis)) * width
    return lax.dynamic_slice_in_dim(doubled, start, n * width, 1)


def small_scatter(value, axis, dim):
    n = lax.axis_size(axis)
    width = value.shape[dim] // n
    me = lax.axis_index(axis)

    def part(k):
        return lax.dynamic_slice_in_dim(value, ((me + k) % n) * width, width, dim)

    return functools.reduce(jnp.add, shifts(part, axis))


def piece_rows(where_ref, s, k, chips, size):
    chip, core = where_ref[0], where_ref[1]
    owner = lax.rem(chip - k + chips, chips)
    other = core if s == 0 else 1 - core
    return pl.multiple_of((2 * owner + other) * size, size)


def head_mask(shape, head):
    lane = lax.broadcasted_iota(jnp.int32, shape, len(shape) - 1)
    return (lane >= head * HD) & (lane < (head + 1) * HD)


def keep_mask(size, start, length):
    key = lax.broadcasted_iota(jnp.int32, (size, size), 0)
    query = lax.broadcasted_iota(jnp.int32, (size, size), 1)
    return (key <= query) & (key + start < length)


def turn(x, cos, plus, minus):
    half = ROT // 2
    width = x.shape[1]
    return x * cos + pltpu.roll(x, half, 1) * plus + pltpu.roll(x, width - half, 1) * minus


def forward_kernel(
    chips, heads, where_ref, own_ref, sib_ref, bias_ref, cos_ref, plus_ref, minus_ref,
    attn_own_ref, attn_sib_ref, qkv_ref, lse_ref, vt_ref, s_ref, attn_ref,
):
    width = heads * HD
    rows = qkv_ref.shape[0]
    size = rows // (2 * chips)
    block = min(256, rows)
    length = where_ref[2]
    for s, half in enumerate((own_ref, sib_ref)):
        for k in range(chips):
            at = pl.ds(piece_rows(where_ref, s, k, chips, size), size)
            raw = half[k * size : (k + 1) * size, :] + bias_ref[...]
            cos, plus, minus = cos_ref[at, :], plus_ref[at, :], minus_ref[at, :]
            for part in range(2):
                x = raw[:, part * width : (part + 1) * width]
                qkv_ref[at, part * width : (part + 1) * width] = turn(x, cos, plus, minus).astype(BF16)
            qkv_ref[at, 2 * width :] = raw[:, 2 * width :].astype(BF16)
    vt_ref[...] = jnp.transpose(qkv_ref[:, 2 * width :])
    for i in range(rows // block):
        here = slice(i * block, (i + 1) * block)
        reach = (i + 1) * block

        @pl.when(i * block < length)
        def _():
            query = qkv_ref[here, :width]
            keys = qkv_ref[:reach, width : 2 * width]
            keep = keep_mask(block, i * block, length)
            pieces = []
            for head in range(heads):
                masked = jnp.where(head_mask(query.shape, head), query, jnp.zeros_like(query))
                s_ref[:reach, :] = dot(keys, masked, 1, 1)
                s_ref[here, :] = jnp.where(keep, s_ref[here, :], NEG)
                scores = s_ref[:reach, :] * (SCALE * LOG2E)
                top = jnp.max(scores, axis=0, keepdims=True)
                weights = jnp.exp2(scores - top)
                total = jnp.sum(weights, axis=0, keepdims=True)
                low = weights.astype(BF16)
                mixed = dot(vt_ref[head * HD : (head + 1) * HD, :reach], low, 1, 0)
                pieces.append(mixed * (1.0 / total))
                lse_ref[head : head + 1, here] = top + jnp.log2(total)
            attn_ref[here, :] = jnp.transpose(jnp.concatenate(pieces, axis=0)).astype(BF16)

        @pl.when(i * block >= length)
        def _():
            attn_ref[here, :] = jnp.zeros((block, width), BF16)
            lse_ref[:, here] = jnp.zeros((lse_ref.shape[0], block), F32)

    for s, half in enumerate((attn_own_ref, attn_sib_ref)):
        for k in range(chips):
            at = pl.ds(piece_rows(where_ref, s, k, chips, size), size)
            half[k * size : (k + 1) * size, :] = attn_ref[at, :]


def backward_kernel(
    chips, heads, where_ref, own_ref, sib_ref, qkv_ref, lse_ref, cos_ref, plus_ref, minus_ref,
    grad_own_ref, grad_sib_ref, bias_grad_ref,
    g_ref, kt_ref, qs_ref, gs_ref, p_ref, d_ref, pcat_ref, scat_ref, dq_ref, dk_ref, dv_ref,
):
    width = heads * HD
    rows = qkv_ref.shape[0]
    size = rows // (2 * chips)
    block = min(256, rows)
    length = where_ref[2]
    for s, half in enumerate((own_ref, sib_ref)):
        for k in range(chips):
            at = pl.ds(piece_rows(where_ref, s, k, chips, size), size)
            g_ref[at, :] = half[k * size : (k + 1) * size, :]
    kt_ref[...] = jnp.transpose(qkv_ref[:, width : 2 * width])
    dk_ref[...] = jnp.zeros_like(dk_ref)
    dv_ref[...] = jnp.zeros_like(dv_ref)
    for i in range(rows // block):
        here = slice(i * block, (i + 1) * block)
        reach = (i + 1) * block

        @pl.when(i * block < length)
        def _():
            query = qkv_ref[here, :width]
            grad = g_ref[here, :]
            keys = qkv_ref[:reach, width : 2 * width]
            values = qkv_ref[:reach, 2 * width :]
            keep = keep_mask(block, i * block, length)
            pieces = []
            for head in range(heads):
                mask = head_mask(query.shape, head)
                cols = slice(head * block, (head + 1) * block)
                qs_ref[cols, :] = jnp.where(mask, query, jnp.zeros_like(query))
                gs_ref[cols, :] = jnp.where(mask, grad, jnp.zeros_like(grad))
                p_ref[:reach, :] = dot(keys, qs_ref[cols, :], 1, 1)
                p_ref[here, :] = jnp.where(keep, p_ref[here, :], NEG)
                weights = jnp.exp2(p_ref[:reach, :] * (SCALE * LOG2E) - lse_ref[head : head + 1, here])
                pcat_ref[:reach, cols] = weights.astype(BF16)
                p_ref[:reach, :] = weights
                d_ref[:reach, :] = dot(values, gs_ref[cols, :], 1, 1)
                offset = jnp.sum(p_ref[:reach, :] * d_ref[:reach, :], axis=0, keepdims=True)
                low = (p_ref[:reach, :] * (d_ref[:reach, :] - offset)).astype(BF16)
                scat_ref[:reach, cols] = low
                pieces.append(dot(kt_ref[head * HD : (head + 1) * HD, :reach], low, 1, 0))
            dv_ref[:reach, :] += dot(pcat_ref[:reach, :], gs_ref[...], 1, 0)
            dk_ref[:reach, :] += dot(scat_ref[:reach, :], qs_ref[...], 1, 0)
            dq_ref[here, :] = jnp.transpose(jnp.concatenate(pieces, axis=0))

        @pl.when(i * block >= length)
        def _():
            dq_ref[here, :] = jnp.zeros((block, width), F32)

    sums = [jnp.zeros((1, width), F32) for _ in range(3)]
    for s, half in enumerate((grad_own_ref, grad_sib_ref)):
        for k in range(chips):
            at = pl.ds(piece_rows(where_ref, s, k, chips, size), size)
            to = slice(k * size, (k + 1) * size)
            cos, plus, minus = cos_ref[at, :], plus_ref[at, :], minus_ref[at, :]
            parts = (
                turn(dq_ref[at, :] * SCALE, cos, -plus, -minus),
                turn(dk_ref[at, :] * SCALE, cos, -plus, -minus),
                dv_ref[at, :],
            )
            for j, part in enumerate(parts):
                low = part.astype(BF16)
                half[to, j * width : (j + 1) * width] = low
                sums[j] = sums[j] + jnp.sum(low.astype(F32), axis=0, keepdims=True)
    bias_grad_ref[...] = jnp.concatenate([jnp.broadcast_to(x, (8, width)) for x in sums], axis=1)


VMEM = pl.BlockSpec(memory_space=pltpu.VMEM)
SMEM = pl.BlockSpec(memory_space=pltpu.SMEM)


def attend(where, own, sib, bias, tables, chips, heads):
    width = heads * HD
    rows = 2 * own.shape[0]
    block = min(256, rows)
    return pl.pallas_call(
        functools.partial(forward_kernel, chips, heads),
        out_shape=(
            jax.ShapeDtypeStruct((rows // 2, width), BF16),
            jax.ShapeDtypeStruct((rows // 2, width), BF16),
            jax.ShapeDtypeStruct((rows, 3 * width), BF16),
            jax.ShapeDtypeStruct((8, rows), F32),
        ),
        in_specs=[SMEM] + [VMEM] * 6,
        out_specs=[VMEM] * 4,
        scratch_shapes=[
            pltpu.VMEM((width, rows), BF16),
            pltpu.VMEM((rows, block), F32),
            pltpu.VMEM((rows, width), BF16),
        ],
        compiler_params=pltpu.CompilerParams(vmem_limit_bytes=32 << 20),
        cost_estimate=pl.CostEstimate(
            flops=heads * rows * rows * 512, transcendentals=heads * rows * rows // 2, bytes_accessed=8 << 20
        ),
        name="attend",
    )(where, own, sib, bias, *tables)


def attend_back(where, own, sib, qkv, lse, tables, chips, heads):
    width = heads * HD
    rows = 2 * own.shape[0]
    block = min(256, rows)
    return pl.pallas_call(
        functools.partial(backward_kernel, chips, heads),
        out_shape=(
            jax.ShapeDtypeStruct((rows // 2, 3 * width), BF16),
            jax.ShapeDtypeStruct((rows // 2, 3 * width), BF16),
            jax.ShapeDtypeStruct((8, 3 * width), F32),
        ),
        in_specs=[SMEM] + [VMEM] * 7,
        out_specs=[VMEM] * 3,
        scratch_shapes=[
            pltpu.VMEM((rows, width), BF16),
            pltpu.VMEM((width, rows), BF16),
            pltpu.VMEM((heads * block, width), BF16),
            pltpu.VMEM((heads * block, width), BF16),
            pltpu.VMEM((rows, block), F32),
            pltpu.VMEM((rows, block), F32),
            pltpu.VMEM((rows, heads * block), BF16),
            pltpu.VMEM((rows, heads * block), BF16),
            pltpu.VMEM((rows, width), F32),
            pltpu.VMEM((rows, width), F32),
            pltpu.VMEM((rows, width), F32),
        ],
        compiler_params=pltpu.CompilerParams(vmem_limit_bytes=40 << 20),
        cost_estimate=pl.CostEstimate(
            flops=heads * rows * rows * 1280, transcendentals=heads * rows * rows // 2, bytes_accessed=8 << 20
        ),
        name="attend_back",
    )(where, own, sib, qkv, lse, *tables)


def rope_tables(rows, width):
    half = ROT // 2
    lane = jnp.arange(width, dtype=jnp.int32) % HD
    power = (lane % half).astype(F32)
    frequency = ROPE_BASE ** (-(2.0 * power) / ROT)
    angles = jnp.arange(rows, dtype=F32)[:, None] * frequency[None, :]
    cos = jnp.where(lane < ROT, jnp.cos(angles), 1.0)
    sine = jnp.sin(angles)
    plus = jnp.where((lane >= half) & (lane < ROT), sine, 0.0)
    minus = jnp.where(lane < half, -sine, 0.0)
    return (cos, plus, minus)


def local(
    tokens,
    out_grad,
    row_seq,
    seq_lengths,
    norm1_gain,
    norm1_bias,
    qkv_weight,
    qk_bias,
    v_bias,
    out_weight,
    norm2_gain,
    norm2_bias,
    gate_weight,
    up_weight,
    down_weight,
):
    line = Line()
    batches, seq_here, rows_here, depth = tokens.shape
    assert rows_here == 1
    chips = line.chips
    seq_full = seq_here * line.devices
    width = qkv_weight.shape[2]
    heads_here = width // HD
    piece = seq_here

    table = jnp.arange(seq_lengths.shape[0], dtype=jnp.int32)
    row_len = jnp.sum(jnp.where(row_seq[..., None] == table, seq_lengths, 0), axis=-1)[:, 0]
    positions = lax.axis_index("heads") * seq_here + jnp.arange(seq_here, dtype=jnp.int32)
    tables = rope_tables(seq_full, width)

    vectors = jnp.stack([norm1_gain, norm1_bias, norm2_gain, norm2_bias])
    vectors = small_gather(small_gather(vectors, "heads").reshape(4, -1), "batch")
    gain_one, shift_one, gain_two, shift_two = (vectors[i] for i in range(4))

    qkv_flat = jnp.concatenate([qkv_weight[:, j] for j in range(3)], axis=1)
    bias = jnp.concatenate([qk_bias[0].reshape(-1), qk_bias[1].reshape(-1), v_bias.reshape(-1)])
    bias = bias.astype(F32)[None, :]
    gate_full = lax.all_gather(gate_weight, "batch", axis=0, tiled=True)
    up_full = lax.all_gather(up_weight, "batch", axis=0, tiled=True)
    down_full = lax.all_gather(down_weight, "batch", axis=0, tiled=True)

    def gather_halves(block):
        own = line.gather(block)
        return (own, line.swap(own))

    def scatter_halves(product):
        received = line.swap(product(1).astype(BF16))
        summed = (product(0) + received.astype(F32)).astype(BF16)
        return line.scatter([summed[k * piece : (k + 1) * piece] for k in range(chips)])

    class Row:
        pass

    rows = []
    for r in range(batches):
        row = Row()
        row.length = row_len[r]
        row.where = jnp.stack([line.chip, line.core, row.length]).astype(jnp.int32)
        row.valid = (positions < row.length).astype(F32)[:, None]
        row.grad_y = (out_grad[r, :, 0].astype(F32) * row.valid).astype(BF16)
        row.inputs = tokens[r, :, 0].astype(F32)
        normed, row.unit_one, row.inverse_one = row_norm(row.inputs, gain_one, shift_one)
        row.normed_one = normed.astype(BF16)
        rows.append(row)

    def stage_attend(row, *earlier):
        raw = [dot(after(x, *earlier), qkv_flat, 1, 0) for x in row.ones]
        *row.attn, row.qkv, row.lse = attend(row.where, *raw, bias, tables, chips, heads_here)
        row.branch = scatter_halves(lambda s: dot(row.attn[s], out_weight, 1, 0))
        return row.attn[0]

    def stage_norm(row, *earlier):
        row.state = row.inputs + after(row.branch, *earlier)
        normed, row.unit_two, row.inverse_two = row_norm(row.state, gain_two, shift_two)
        row.normed_two = normed.astype(BF16)
        row.twos = gather_halves(row.normed_two)
        return row.normed_two

    def stage_mlp(row, *earlier):
        row.inner, row.grad_gate, row.grad_up = [], [], []
        for s in range(2):
            twos = after(row.twos[s], *earlier)
            gate = dot(twos, gate_full, 1, 0)
            up = dot(twos, up_full, 1, 0)
            sigma = jax.nn.sigmoid(gate)
            silu = gate * sigma
            row.inner.append((silu * up).astype(BF16))
            grad_inner = dot(row.grads[s], down_full, 1, 0)
            row.grad_gate.append((grad_inner * up * sigma * (1.0 + gate * (1.0 - sigma))).astype(BF16))
            row.grad_up.append((grad_inner * silu).astype(BF16))
        row.grad_two = scatter_halves(
            lambda s: dot(row.grad_gate[s], gate_full, 1, 1) + dot(row.grad_up[s], up_full, 1, 1)
        )
        return row.grad_gate[0]

    def stage_state(row, *earlier):
        row.grad_two = after(row.grad_two, *earlier)
        row.grad_state = row.grad_y.astype(F32) + norm_back(
            row.grad_two, row.unit_two, row.inverse_two, gain_two
        )
        low = row.grad_state.astype(BF16)
        row.states = gather_halves(low)
        return low

    def stage_back(row, *earlier):
        grad_attn = [dot(after(x, *earlier), out_weight, 1, 1).astype(BF16) for x in row.states]
        *row.grad_qkv, bias_grad = attend_back(
            row.where, *grad_attn, row.qkv, row.lse, tables, chips, heads_here
        )
        row.bias_grad = bias_grad[0]
        row.grad_one = scatter_halves(lambda s: dot(row.grad_qkv[s], qkv_flat, 1, 1))
        return row.grad_qkv[0]

    def stage_down(row, *earlier):
        row.inner = [after(x, *earlier) for x in row.inner]
        row.mlp = scatter_halves(lambda s: dot(row.inner[s], down_full, 1, 1))

    def stage_end(row):
        row.input_grad = row.grad_state + norm_back(
            row.grad_one, row.unit_one, row.inverse_one, gain_one
        )
        row.norms = jnp.stack(
            [
                jnp.sum(row.grad_one * row.unit_one, axis=0),
                jnp.sum(row.grad_one, axis=0),
                jnp.sum(row.grad_two * row.unit_two, axis=0),
                jnp.sum(row.grad_two, axis=0),
            ]
        )
        row.output = ((row.state + row.mlp) * row.valid).astype(BF16)

    first, second = rows
    for row in rows:
        row.ones = gather_halves(row.normed_one)
        row.grads = gather_halves(row.grad_y)
    token = stage_attend(first)
    token = stage_attend(second, token)
    token = stage_norm(first, token)
    token = stage_norm(second, token)
    token = stage_mlp(first, token)
    token = stage_mlp(second, token)
    stage_down(first, token)
    stage_down(second, token)
    token = stage_state(first, token)
    token = stage_state(second, token)
    token = stage_back(first, token)
    token = stage_back(second, token)
    for row in rows:
        stage_end(row)

    def weight_grad(left, right, dim):
        total = None
        for row in rows:
            for s in range(2):
                term = dot(getattr(row, left)[s], getattr(row, right)[s], 0, 0)
                total = term if total is None else total + term
        low = total.astype(BF16)
        return lax.psum_scatter(low, "batch", scatter_dimension=dim, tiled=True).astype(F32)

    down_grad = weight_grad("grads", "inner", 0)
    gate_grad = weight_grad("twos", "grad_gate", 0)
    up_grad = weight_grad("twos", "grad_up", 0)
    out_grad_w = weight_grad("attn", "states", 1)
    qkv_grad = weight_grad("ones", "grad_qkv", 0)
    qkv_grad = jnp.stack([qkv_grad[:, j * width : (j + 1) * width] for j in range(3)], axis=1)

    bias_sum = functools.reduce(jnp.add, [row.bias_grad for row in rows])
    bias_sum = small_scatter(bias_sum.reshape(3 * heads_here, HD), "batch", 1)
    bias_sum = bias_sum.reshape(3, heads_here, -1)
    norm_sum = functools.reduce(jnp.add, [row.norms for row in rows])
    norm_sum = small_scatter(small_scatter(norm_sum, "batch", 1), "heads", 1)
    return (
        jnp.stack([row.output for row in rows])[:, :, None],
        jnp.stack([row.input_grad.astype(BF16) for row in rows])[:, :, None],
        norm_sum[0],
        norm_sum[1],
        qkv_grad,
        bias_sum[:2],
        bias_sum[2],
        out_grad_w,
        norm_sum[2],
        norm_sum[3],
        gate_grad,
        up_grad,
        down_grad,
    )


def solution(mesh):
    placed = (
        P(None, "heads", "batch", None),
        P(None, "heads", "batch", None),
        P(None, "batch"),
        P(),
        P(("batch", "heads")),
        P(("batch", "heads")),
        P(None, None, "heads"),
        P(None, "heads", None),
        P("heads", None),
        P("heads", None),
        P(("batch", "heads")),
        P(("batch", "heads")),
        P("batch", "heads"),
        P("batch", "heads"),
        P("batch", "heads"),
    )
    return jax.shard_map(
        local,
        mesh=mesh,
        in_specs=placed,
        out_specs=(
            P(None, "heads", "batch", None),
            P(None, "heads", "batch", None),
            P(("batch", "heads")),
            P(("batch", "heads")),
            P("batch", None, "heads"),
            P(None, "heads", "batch"),
            P("heads", "batch"),
            P("heads", "batch"),
            P(("batch", "heads")),
            P(("batch", "heads")),
            P("batch", "heads"),
            P("batch", "heads"),
            P("batch", "heads"),
        ),
        check_vma=False,
    )
```

```python
import functools
import math

import jax
import jax.numpy as jnp
from jax import lax
from jax.experimental import pallas as pl
from jax.experimental.pallas import tpu as pltpu
from jax.sharding import PartitionSpec as P

HD = 64
ROT = 16
EPS = 1e-05
NEG = -1e30
ROPE_BASE = 10000.0
SCALE = HD ** (-0.5)
LOG2E = math.log2(math.e)
F32 = jnp.float32
BF16 = jnp.bfloat16


def dot(a, b, ca, cb):
    return lax.dot_general(a, b, (((ca,), (cb,)), ((), ())), preferred_element_type=F32)


def row_norm(values, gain_vec, shift_vec):
    average = jnp.mean(values, axis=-1, keepdims=True)
    centred = values - average
    inverse = lax.rsqrt(jnp.mean(centred * centred, axis=-1, keepdims=True) + EPS)
    unit_rows = centred * inverse
    return (unit_rows * gain_vec + shift_vec, unit_rows, inverse)


def norm_back(gradient, unit_rows, inverse, gain_vec):
    scaled_grad = gradient * gain_vec
    return inverse * (
        scaled_grad
        - jnp.mean(scaled_grad, axis=-1, keepdims=True)
        - unit_rows * jnp.mean(scaled_grad * unit_rows, axis=-1, keepdims=True)
    )


class Line:
    def __init__(self):
        self.devices = lax.axis_size("heads")
        self.chips = self.devices // 2
        index = lax.axis_index("heads")
        self.chip = index // 2
        self.core = index % 2

    def hop(self, value, sources, step):
        pairs = [(2 * i + c, 2 * (i + step) + c) for i in sources for c in range(2)]
        return lax.ppermute(value, "heads", pairs)

    def swap(self, value):
        pairs = [(2 * i + c, 2 * i + 1 - c) for i in range(self.chips) for c in range(2)]
        return lax.ppermute(value, "heads", pairs)

    def place(self, k, core):
        return 2 * ((self.chip - k) % self.chips) + core

    def pick(self, full):
        size = full.shape[0] // self.devices
        return tuple(
            jnp.concatenate(
                [lax.dynamic_slice_in_dim(full, self.place(k, core) * size, size, 0) for k in range(self.chips)]
            )
            for core in (self.core, 1 - self.core)
        )

    def spread(self, halves):
        size = halves[0].shape[0] // self.chips
        full = jnp.zeros((size * self.devices, halves[0].shape[1]), halves[0].dtype)
        for half, core in zip(halves, (self.core, 1 - self.core)):
            for k in range(self.chips):
                rows = half[k * size : (k + 1) * size]
                full = lax.dynamic_update_slice_in_dim(full, rows, self.place(k, core) * size, 0)
        return full

    def gather(self, block):
        n = self.chips
        ups, downs = [block], [block]
        for step in range(1, n):
            ups.append(self.hop(ups[-1], range(step - 1, n - 1), 1))
            downs.append(self.hop(downs[-1], range(1, n - step + 1), -1))
        pieces = [block]
        for k in range(1, n):
            pieces.append(jnp.where(self.chip >= k, ups[k], downs[n - k]))
        return jnp.concatenate(pieces, axis=0)

    def scatter(self, pieces):
        n = self.chips
        up = down = None
        for m in range(n - 1, 0, -1):
            value_up = pieces[n - m] if up is None else add_low(pieces[n - m], up)
            value_down = pieces[m] if down is None else add_low(pieces[m], down)
            up = self.hop(value_up, range(0, n - m), 1)
            down = self.hop(value_down, range(m, n), -1)
        return pieces[0].astype(F32) + up.astype(F32) + down.astype(F32)


def after(value, *earlier):
    return lax.optimization_barrier((value, *earlier))[0]


def add_low(a, b):
    return (a.astype(F32) + b.astype(F32)).astype(BF16)


def shifts(value_of, axis):
    n = lax.axis_size(axis)
    received = [value_of(0)]
    for k in range(1, n):
        received.append(lax.ppermute(value_of(k), axis, [(i, (i + k) % n) for i in range(n)]))
    return received


def small_gather(value, axis):
    n = lax.axis_size(axis)
    received = shifts(lambda k: value, axis)
    width = value.shape[1]
    ordered = jnp.concatenate(received[::-1], axis=1)
    doubled = jnp.concatenate([ordered, ordered], axis=1)
    start = (n - 1 - lax.axis_index(axis)) * width
    return lax.dynamic_slice_in_dim(doubled, start, n * width, 1)


def small_scatter(value, axis, dim):
    n = lax.axis_size(axis)
    width = value.shape[dim] // n
    me = lax.axis_index(axis)

    def part(k):
        return lax.dynamic_slice_in_dim(value, ((me + k) % n) * width, width, dim)

    return functools.reduce(jnp.add, shifts(part, axis))


def piece_rows(where_ref, s, k, chips, size):
    chip, core = where_ref[0], where_ref[1]
    owner = lax.rem(chip - k + chips, chips)
    other = core if s == 0 else 1 - core
    return pl.multiple_of((2 * owner + other) * size, size)


def head_mask(shape, head):
    lane = lax.broadcasted_iota(jnp.int32, shape, len(shape) - 1)
    return (lane >= head * HD) & (lane < (head + 1) * HD)


def keep_mask(size, start, length):
    key = lax.broadcasted_iota(jnp.int32, (size, size), 0)
    query = lax.broadcasted_iota(jnp.int32, (size, size), 1)
    return (key <= query) & (key + start < length)


def turn(x, cos, plus, minus):
    half = ROT // 2
    width = x.shape[1]
    return x * cos + pltpu.roll(x, half, 1) * plus + pltpu.roll(x, width - half, 1) * minus


def forward_kernel(
    chips, heads, where_ref, own_ref, sib_ref, bias_ref, cos_ref, plus_ref, minus_ref,
    attn_own_ref, attn_sib_ref, qkv_ref, lse_ref, vt_ref, s_ref, attn_ref,
):
    width = heads * HD
    rows = qkv_ref.shape[0]
    size = rows // (2 * chips)
    block = min(256, rows)
    length = where_ref[2]
    for s, half in enumerate((own_ref, sib_ref)):
        for k in range(chips):
            at = pl.ds(piece_rows(where_ref, s, k, chips, size), size)
            raw = half[k * size : (k + 1) * size, :] + bias_ref[...]
            cos, plus, minus = cos_ref[at, :], plus_ref[at, :], minus_ref[at, :]
            for part in range(2):
                x = raw[:, part * width : (part + 1) * width]
                qkv_ref[at, part * width : (part + 1) * width] = turn(x, cos, plus, minus).astype(BF16)
            qkv_ref[at, 2 * width :] = raw[:, 2 * width :].astype(BF16)
    vt_ref[...] = jnp.transpose(qkv_ref[:, 2 * width :])
    for i in range(rows // block):
        here = slice(i * block, (i + 1) * block)
        reach = (i + 1) * block

        @pl.when(i * block < length)
        def _():
            query = qkv_ref[here, :width]
            keys = qkv_ref[:reach, width : 2 * width]
            keep = keep_mask(block, i * block, length)
            pieces = []
            for head in range(heads):
                masked = jnp.where(head_mask(query.shape, head), query, jnp.zeros_like(query))
                s_ref[:reach, :] = dot(keys, masked, 1, 1)
                s_ref[here, :] = jnp.where(keep, s_ref[here, :], NEG)
                scores = s_ref[:reach, :] * (SCALE * LOG2E)
                top = jnp.max(scores, axis=0, keepdims=True)
                weights = jnp.exp2(scores - top)
                total = jnp.sum(weights, axis=0, keepdims=True)
                low = weights.astype(BF16)
                mixed = dot(vt_ref[head * HD : (head + 1) * HD, :reach], low, 1, 0)
                pieces.append(mixed * (1.0 / total))
                lse_ref[head : head + 1, here] = top + jnp.log2(total)
            attn_ref[here, :] = jnp.transpose(jnp.concatenate(pieces, axis=0)).astype(BF16)

        @pl.when(i * block >= length)
        def _():
            attn_ref[here, :] = jnp.zeros((block, width), BF16)
            lse_ref[:, here] = jnp.zeros((lse_ref.shape[0], block), F32)

    for s, half in enumerate((attn_own_ref, attn_sib_ref)):
        for k in range(chips):
            at = pl.ds(piece_rows(where_ref, s, k, chips, size), size)
            half[k * size : (k + 1) * size, :] = attn_ref[at, :]


def backward_kernel(
    chips, heads, where_ref, own_ref, sib_ref, qkv_ref, lse_ref, cos_ref, plus_ref, minus_ref,
    grad_own_ref, grad_sib_ref, bias_grad_ref,
    g_ref, kt_ref, qs_ref, gs_ref, p_ref, d_ref, pcat_ref, scat_ref, dq_ref, dk_ref, dv_ref,
):
    width = heads * HD
    rows = qkv_ref.shape[0]
    size = rows // (2 * chips)
    block = min(256, rows)
    length = where_ref[2]
    for s, half in enumerate((own_ref, sib_ref)):
        for k in range(chips):
            at = pl.ds(piece_rows(where_ref, s, k, chips, size), size)
            g_ref[at, :] = half[k * size : (k + 1) * size, :]
    kt_ref[...] = jnp.transpose(qkv_ref[:, width : 2 * width])
    dk_ref[...] = jnp.zeros_like(dk_ref)
    dv_ref[...] = jnp.zeros_like(dv_ref)
    for i in range(rows // block):
        here = slice(i * block, (i + 1) * block)
        reach = (i + 1) * block

        @pl.when(i * block < length)
        def _():
            query = qkv_ref[here, :width]
            grad = g_ref[here, :]
            keys = qkv_ref[:reach, width : 2 * width]
            values = qkv_ref[:reach, 2 * width :]
            keep = keep_mask(block, i * block, length)
            pieces = []
            for head in range(heads):
                mask = head_mask(query.shape, head)
                cols = slice(head * block, (head + 1) * block)
                qs_ref[cols, :] = jnp.where(mask, query, jnp.zeros_like(query))
                gs_ref[cols, :] = jnp.where(mask, grad, jnp.zeros_like(grad))
                p_ref[:reach, :] = dot(keys, qs_ref[cols, :], 1, 1)
                p_ref[here, :] = jnp.where(keep, p_ref[here, :], NEG)
                weights = jnp.exp2(p_ref[:reach, :] * (SCALE * LOG2E) - lse_ref[head : head + 1, here])
                pcat_ref[:reach, cols] = weights.astype(BF16)
                p_ref[:reach, :] = weights
                d_ref[:reach, :] = dot(values, gs_ref[cols, :], 1, 1)
                offset = jnp.sum(p_ref[:reach, :] * d_ref[:reach, :], axis=0, keepdims=True)
                low = (p_ref[:reach, :] * (d_ref[:reach, :] - offset)).astype(BF16)
                scat_ref[:reach, cols] = low
                pieces.append(dot(kt_ref[head * HD : (head + 1) * HD, :reach], low, 1, 0))
            dv_ref[:reach, :] += dot(pcat_ref[:reach, :], gs_ref[...], 1, 0)
            dk_ref[:reach, :] += dot(scat_ref[:reach, :], qs_ref[...], 1, 0)
            dq_ref[here, :] = jnp.transpose(jnp.concatenate(pieces, axis=0))

        @pl.when(i * block >= length)
        def _():
            dq_ref[here, :] = jnp.zeros((block, width), F32)

    sums = [jnp.zeros((1, width), F32) for _ in range(3)]
    for s, half in enumerate((grad_own_ref, grad_sib_ref)):
        for k in range(chips):
            at = pl.ds(piece_rows(where_ref, s, k, chips, size), size)
            to = slice(k * size, (k + 1) * size)
            cos, plus, minus = cos_ref[at, :], plus_ref[at, :], minus_ref[at, :]
            parts = (
                turn(dq_ref[at, :] * SCALE, cos, -plus, -minus),
                turn(dk_ref[at, :] * SCALE, cos, -plus, -minus),
                dv_ref[at, :],
            )
            for j, part in enumerate(parts):
                low = part.astype(BF16)
                half[to, j * width : (j + 1) * width] = low
                sums[j] = sums[j] + jnp.sum(low.astype(F32), axis=0, keepdims=True)
    bias_grad_ref[...] = jnp.concatenate([jnp.broadcast_to(x, (8, width)) for x in sums], axis=1)


VMEM = pl.BlockSpec(memory_space=pltpu.VMEM)
SMEM = pl.BlockSpec(memory_space=pltpu.SMEM)


def attend(where, own, sib, bias, tables, chips, heads):
    width = heads * HD
    rows = 2 * own.shape[0]
    block = min(256, rows)
    return pl.pallas_call(
        functools.partial(forward_kernel, chips, heads),
        out_shape=(
            jax.ShapeDtypeStruct((rows // 2, width), BF16),
            jax.ShapeDtypeStruct((rows // 2, width), BF16),
            jax.ShapeDtypeStruct((rows, 3 * width), BF16),
            jax.ShapeDtypeStruct((8, rows), F32),
        ),
        in_specs=[SMEM] + [VMEM] * 6,
        out_specs=[VMEM] * 4,
        scratch_shapes=[
            pltpu.VMEM((width, rows), BF16),
            pltpu.VMEM((rows, block), F32),
            pltpu.VMEM((rows, width), BF16),
        ],
        compiler_params=pltpu.CompilerParams(vmem_limit_bytes=32 << 20),
        cost_estimate=pl.CostEstimate(
            flops=heads * rows * rows * 512, transcendentals=heads * rows * rows // 2, bytes_accessed=8 << 20
        ),
        name="attend",
    )(where, own, sib, bias, *tables)


def attend_back(where, own, sib, qkv, lse, tables, chips, heads):
    width = heads * HD
    rows = 2 * own.shape[0]
    block = min(256, rows)
    return pl.pallas_call(
        functools.partial(backward_kernel, chips, heads),
        out_shape=(
            jax.ShapeDtypeStruct((rows // 2, 3 * width), BF16),
            jax.ShapeDtypeStruct((rows // 2, 3 * width), BF16),
            jax.ShapeDtypeStruct((8, 3 * width), F32),
        ),
        in_specs=[SMEM] + [VMEM] * 7,
        out_specs=[VMEM] * 3,
        scratch_shapes=[
            pltpu.VMEM((rows, width), BF16),
            pltpu.VMEM((width, rows), BF16),
            pltpu.VMEM((heads * block, width), BF16),
            pltpu.VMEM((heads * block, width), BF16),
            pltpu.VMEM((rows, block), F32),
            pltpu.VMEM((rows, block), F32),
            pltpu.VMEM((rows, heads * block), BF16),
            pltpu.VMEM((rows, heads * block), BF16),
            pltpu.VMEM((rows, width), F32),
            pltpu.VMEM((rows, width), F32),
            pltpu.VMEM((rows, width), F32),
        ],
        compiler_params=pltpu.CompilerParams(vmem_limit_bytes=40 << 20),
        cost_estimate=pl.CostEstimate(
            flops=heads * rows * rows * 1280, transcendentals=heads * rows * rows // 2, bytes_accessed=8 << 20
        ),
        name="attend_back",
    )(where, own, sib, qkv, lse, *tables)


def rope_tables(rows, width):
    half = ROT // 2
    lane = jnp.arange(width, dtype=jnp.int32) % HD
    power = (lane % half).astype(F32)
    frequency = ROPE_BASE ** (-(2.0 * power) / ROT)
    angles = jnp.arange(rows, dtype=F32)[:, None] * frequency[None, :]
    cos = jnp.where(lane < ROT, jnp.cos(angles), 1.0)
    sine = jnp.sin(angles)
    plus = jnp.where((lane >= half) & (lane < ROT), sine, 0.0)
    minus = jnp.where(lane < half, -sine, 0.0)
    return (cos, plus, minus)


def local(
    tokens,
    out_grad,
    row_seq,
    seq_lengths,
    norm1_gain,
    norm1_bias,
    qkv_weight,
    qk_bias,
    v_bias,
    out_weight,
    norm2_gain,
    norm2_bias,
    gate_weight,
    up_weight,
    down_weight,
):
    line = Line()
    batches, seq_here, rows_here, depth = tokens.shape
    assert rows_here == 1
    chips = line.chips
    seq_full = seq_here * line.devices
    width = qkv_weight.shape[2]
    heads_here = width // HD
    piece = seq_here

    table = jnp.arange(seq_lengths.shape[0], dtype=jnp.int32)
    row_len = jnp.sum(jnp.where(row_seq[..., None] == table, seq_lengths, 0), axis=-1)[:, 0]
    positions = lax.axis_index("heads") * seq_here + jnp.arange(seq_here, dtype=jnp.int32)
    tables = rope_tables(seq_full, width)

    vectors = jnp.stack([norm1_gain, norm1_bias, norm2_gain, norm2_bias])
    vectors = small_gather(small_gather(vectors, "heads").reshape(4, -1), "batch")
    gain_one, shift_one, gain_two, shift_two = (vectors[i] for i in range(4))

    qkv_flat = jnp.concatenate([qkv_weight[:, j] for j in range(3)], axis=1)
    bias = jnp.concatenate([qk_bias[0].reshape(-1), qk_bias[1].reshape(-1), v_bias.reshape(-1)])
    bias = bias.astype(F32)[None, :]
    gate_full = lax.all_gather(gate_weight, "batch", axis=0, tiled=True)
    up_full = lax.all_gather(up_weight, "batch", axis=0, tiled=True)
    down_full = lax.all_gather(down_weight, "batch", axis=0, tiled=True)

    def gather_halves(block):
        own = line.gather(block)
        return (own, line.swap(own))

    def scatter_halves(product):
        received = line.swap(product(1).astype(BF16))
        summed = (product(0) + received.astype(F32)).astype(BF16)
        return line.scatter([summed[k * piece : (k + 1) * piece] for k in range(chips)])

    class Row:
        pass

    rows = []
    for r in range(batches):
        row = Row()
        row.length = row_len[r]
        row.where = jnp.stack([line.chip, line.core, row.length]).astype(jnp.int32)
        row.valid = (positions < row.length).astype(F32)[:, None]
        row.grad_y = (out_grad[r, :, 0].astype(F32) * row.valid).astype(BF16)
        row.inputs = tokens[r, :, 0].astype(F32)
        normed, row.unit_one, row.inverse_one = row_norm(row.inputs, gain_one, shift_one)
        row.normed_one = normed.astype(BF16)
        rows.append(row)

    def stage_attend(row, *earlier):
        raw = [dot(after(x, *earlier), qkv_flat, 1, 0) for x in row.ones]
        *row.attn, row.qkv, row.lse = attend(row.where, *raw, bias, tables, chips, heads_here)
        row.branch = scatter_halves(lambda s: dot(row.attn[s], out_weight, 1, 0))
        return row.attn[0]

    def stage_norm(row, *earlier):
        row.state = row.inputs + after(row.branch, *earlier)
        normed, row.unit_two, row.inverse_two = row_norm(row.state, gain_two, shift_two)
        row.normed_two = normed.astype(BF16)
        row.twos = gather_halves(row.normed_two)
        return row.normed_two

    def stage_mlp(row, *earlier):
        row.inner, row.grad_gate, row.grad_up = [], [], []
        for s in range(2):
            twos = after(row.twos[s], *earlier)
            gate = dot(twos, gate_full, 1, 0)
            up = dot(twos, up_full, 1, 0)
            sigma = jax.nn.sigmoid(gate)
            silu = gate * sigma
            row.inner.append((silu * up).astype(BF16))
            grad_inner = dot(row.grads[s], down_full, 1, 0)
            row.grad_gate.append((grad_inner * up * sigma * (1.0 + gate * (1.0 - sigma))).astype(BF16))
            row.grad_up.append((grad_inner * silu).astype(BF16))
        row.grad_two = scatter_halves(
            lambda s: dot(row.grad_gate[s], gate_full, 1, 1) + dot(row.grad_up[s], up_full, 1, 1)
        )
        return row.grad_gate[0]

    def stage_state(row, *earlier):
        row.grad_two = after(row.grad_two, *earlier)
        row.grad_state = row.grad_y.astype(F32) + norm_back(
            row.grad_two, row.unit_two, row.inverse_two, gain_two
        )
        low = row.grad_state.astype(BF16)
        row.states = gather_halves(low)
        return low

    def stage_back(row, *earlier):
        grad_attn = [dot(after(x, *earlier), out_weight, 1, 1).astype(BF16) for x in row.states]
        *row.grad_qkv, bias_grad = attend_back(
            row.where, *grad_attn, row.qkv, row.lse, tables, chips, heads_here
        )
        row.bias_grad = bias_grad[0]
        row.grad_one = scatter_halves(lambda s: dot(row.grad_qkv[s], qkv_flat, 1, 1))
        return row.grad_qkv[0]

    def stage_down(row, *earlier):
        inner = line.spread([after(x, *earlier) for x in row.inner])
        low = dot(inner, down_full, 1, 1).astype(BF16)
        row.mlp = lax.psum_scatter(low, "heads", scatter_dimension=0, tiled=True).astype(F32)

    def stage_end(row):
        row.input_grad = row.grad_state + norm_back(
            row.grad_one, row.unit_one, row.inverse_one, gain_one
        )
        row.norms = jnp.stack(
            [
                jnp.sum(row.grad_one * row.unit_one, axis=0),
                jnp.sum(row.grad_one, axis=0),
                jnp.sum(row.grad_two * row.unit_two, axis=0),
                jnp.sum(row.grad_two, axis=0),
            ]
        )
        row.output = ((row.state + row.mlp) * row.valid).astype(BF16)

    first, second = rows
    for row in rows:
        row.ones = gather_halves(row.normed_one)
        row.grads = line.pick(lax.all_gather(row.grad_y, "heads", axis=0, tiled=True))
    token = stage_attend(first)
    token = stage_attend(second, token)
    token = stage_norm(first, token)
    token = stage_norm(second, token)
    token = stage_mlp(first, token)
    token = stage_mlp(second, token)
    stage_down(first, token)
    stage_down(second, token)
    token = stage_state(first, token)
    token = stage_state(second, token)
    token = stage_back(first, token)
    token = stage_back(second, token)
    for row in rows:
        stage_end(row)

    def weight_grad(left, right, dim):
        total = None
        for row in rows:
            for s in range(2):
                term = dot(getattr(row, left)[s], getattr(row, right)[s], 0, 0)
                total = term if total is None else total + term
        low = total.astype(BF16)
        return lax.psum_scatter(low, "batch", scatter_dimension=dim, tiled=True).astype(F32)

    down_grad = weight_grad("grads", "inner", 0)
    gate_grad = weight_grad("twos", "grad_gate", 0)
    up_grad = weight_grad("twos", "grad_up", 0)
    out_grad_w = weight_grad("attn", "states", 1)
    qkv_grad = weight_grad("ones", "grad_qkv", 0)
    qkv_grad = jnp.stack([qkv_grad[:, j * width : (j + 1) * width] for j in range(3)], axis=1)

    bias_sum = functools.reduce(jnp.add, [row.bias_grad for row in rows])
    bias_sum = small_scatter(bias_sum.reshape(3 * heads_here, HD), "batch", 1)
    bias_sum = bias_sum.reshape(3, heads_here, -1)
    norm_sum = functools.reduce(jnp.add, [row.norms for row in rows])
    norm_sum = small_scatter(small_scatter(norm_sum, "batch", 1), "heads", 1)
    return (
        jnp.stack([row.output for row in rows])[:, :, None],
        jnp.stack([row.input_grad.astype(BF16) for row in rows])[:, :, None],
        norm_sum[0],
        norm_sum[1],
        qkv_grad,
        bias_sum[:2],
        bias_sum[2],
        out_grad_w,
        norm_sum[2],
        norm_sum[3],
        gate_grad,
        up_grad,
        down_grad,
    )


def solution(mesh):
    placed = (
        P(None, "heads", "batch", None),
        P(None, "heads", "batch", None),
        P(None, "batch"),
        P(),
        P(("batch", "heads")),
        P(("batch", "heads")),
        P(None, None, "heads"),
        P(None, "heads", None),
        P("heads", None),
        P("heads", None),
        P(("batch", "heads")),
        P(("batch", "heads")),
        P("batch", "heads"),
        P("batch", "heads"),
        P("batch", "heads"),
    )
    return jax.shard_map(
        local,
        mesh=mesh,
        in_specs=placed,
        out_specs=(
            P(None, "heads", "batch", None),
            P(None, "heads", "batch", None),
            P(("batch", "heads")),
            P(("batch", "heads")),
            P("batch", None, "heads"),
            P(None, "heads", "batch"),
            P("heads", "batch"),
            P("heads", "batch"),
            P(("batch", "heads")),
            P(("batch", "heads")),
            P("batch", "heads"),
            P("batch", "heads"),
            P("batch", "heads"),
        ),
        check_vma=False,
    )
```

```python
import functools
import math

import jax
import jax.numpy as jnp
from jax import lax
from jax.experimental import pallas as pl
from jax.experimental.pallas import tpu as pltpu
from jax.sharding import PartitionSpec as P

HD = 64
ROT = 16
EPS = 1e-05
NEG = -1e30
ROPE_BASE = 10000.0
SCALE = HD ** (-0.5)
LOG2E = math.log2(math.e)
F32 = jnp.float32
BF16 = jnp.bfloat16


def dot(a, b, ca, cb):
    return lax.dot_general(a, b, (((ca,), (cb,)), ((), ())), preferred_element_type=F32)


def row_norm(values, gain_vec, shift_vec):
    average = jnp.mean(values, axis=-1, keepdims=True)
    centred = values - average
    inverse = lax.rsqrt(jnp.mean(centred * centred, axis=-1, keepdims=True) + EPS)
    unit_rows = centred * inverse
    return (unit_rows * gain_vec + shift_vec, unit_rows, inverse)


def norm_back(gradient, unit_rows, inverse, gain_vec):
    scaled_grad = gradient * gain_vec
    return inverse * (
        scaled_grad
        - jnp.mean(scaled_grad, axis=-1, keepdims=True)
        - unit_rows * jnp.mean(scaled_grad * unit_rows, axis=-1, keepdims=True)
    )


class Line:
    def __init__(self):
        self.devices = lax.axis_size("heads")
        self.chips = self.devices // 2
        index = lax.axis_index("heads")
        self.chip = index // 2
        self.core = index % 2

    def hop(self, value, sources, step):
        pairs = [(2 * i + c, 2 * (i + step) + c) for i in sources for c in range(2)]
        return lax.ppermute(value, "heads", pairs)

    def swap(self, value):
        pairs = [(2 * i + c, 2 * i + 1 - c) for i in range(self.chips) for c in range(2)]
        return lax.ppermute(value, "heads", pairs)

    def place(self, k, core):
        return 2 * ((self.chip - k) % self.chips) + core

    def pick(self, full):
        size = full.shape[0] // self.devices
        return tuple(
            jnp.concatenate(
                [lax.dynamic_slice_in_dim(full, self.place(k, core) * size, size, 0) for k in range(self.chips)]
            )
            for core in (self.core, 1 - self.core)
        )

    def spread(self, halves):
        size = halves[0].shape[0] // self.chips
        full = jnp.zeros((size * self.devices, halves[0].shape[1]), halves[0].dtype)
        for half, core in zip(halves, (self.core, 1 - self.core)):
            for k in range(self.chips):
                rows = half[k * size : (k + 1) * size]
                full = lax.dynamic_update_slice_in_dim(full, rows, self.place(k, core) * size, 0)
        return full

    def gather(self, block):
        n = self.chips
        ups, downs = [block], [block]
        for step in range(1, n):
            ups.append(self.hop(ups[-1], range(step - 1, n - 1), 1))
            downs.append(self.hop(downs[-1], range(1, n - step + 1), -1))
        pieces = [block]
        for k in range(1, n):
            pieces.append(jnp.where(self.chip >= k, ups[k], downs[n - k]))
        return jnp.concatenate(pieces, axis=0)

    def scatter(self, pieces):
        n = self.chips
        up = down = None
        for m in range(n - 1, 0, -1):
            value_up = pieces[n - m] if up is None else add_low(pieces[n - m], up)
            value_down = pieces[m] if down is None else add_low(pieces[m], down)
            up = self.hop(value_up, range(0, n - m), 1)
            down = self.hop(value_down, range(m, n), -1)
        return pieces[0].astype(F32) + up.astype(F32) + down.astype(F32)


def after(value, *earlier):
    return lax.optimization_barrier((value, *earlier))[0]


def add_low(a, b):
    return (a.astype(F32) + b.astype(F32)).astype(BF16)


def ring(axis, group):
    size, index = lax.axis_size(axis), lax.axis_index(axis)
    if group == "core":
        return 2, index % 2, lambda k: [(i, i ^ k) for i in range(size)]
    if group == "chip":
        return size // 2, index // 2, lambda k: [(i, (i + 2 * k) % size) for i in range(size)]
    return size, index, lambda k: [(i, (i + k) % size) for i in range(size)]


def shifts(value_of, axis, group):
    n, _, pairs = ring(axis, group)
    return [value_of(0)] + [lax.ppermute(value_of(k), axis, pairs(k)) for k in range(1, n)]


def small_gather(value, axis, group="all"):
    n, me, _ = ring(axis, group)
    received = shifts(lambda k: value, axis, group)
    width = value.shape[1]
    ordered = jnp.concatenate(received[::-1], axis=1)
    doubled = jnp.concatenate([ordered, ordered], axis=1)
    return lax.dynamic_slice_in_dim(doubled, (n - 1 - me) * width, n * width, 1)


def small_scatter(value, axis, dim, group="all"):
    n, me, _ = ring(axis, group)
    width = value.shape[dim] // n

    def part(k):
        return lax.dynamic_slice_in_dim(value, ((me + k) % n) * width, width, dim)

    return functools.reduce(jnp.add, shifts(part, axis, group))


def piece_rows(where_ref, s, k, chips, size):
    chip, core = where_ref[0], where_ref[1]
    owner = lax.rem(chip - k + chips, chips)
    other = core if s == 0 else 1 - core
    return pl.multiple_of((2 * owner + other) * size, size)


def head_mask(shape, head):
    lane = lax.broadcasted_iota(jnp.int32, shape, len(shape) - 1)
    return (lane >= head * HD) & (lane < (head + 1) * HD)


def keep_mask(size, start, length):
    key = lax.broadcasted_iota(jnp.int32, (size, size), 0)
    query = lax.broadcasted_iota(jnp.int32, (size, size), 1)
    return (key <= query) & (key + start < length)


def turn(x, cos, plus, minus):
    half = ROT // 2
    width = x.shape[1]
    return x * cos + pltpu.roll(x, half, 1) * plus + pltpu.roll(x, width - half, 1) * minus


def forward_kernel(
    chips, heads, where_ref, own_ref, sib_ref, bias_ref, cos_ref, plus_ref, minus_ref,
    attn_own_ref, attn_sib_ref, qkv_ref, lse_ref, vt_ref, s_ref, attn_ref,
):
    width = heads * HD
    rows = qkv_ref.shape[0]
    size = rows // (2 * chips)
    block = min(256, rows)
    length = where_ref[2]
    for s, half in enumerate((own_ref, sib_ref)):
        for k in range(chips):
            at = pl.ds(piece_rows(where_ref, s, k, chips, size), size)
            raw = half[k * size : (k + 1) * size, :] + bias_ref[...]
            cos, plus, minus = cos_ref[at, :], plus_ref[at, :], minus_ref[at, :]
            for part in range(2):
                x = raw[:, part * width : (part + 1) * width]
                qkv_ref[at, part * width : (part + 1) * width] = turn(x, cos, plus, minus).astype(BF16)
            qkv_ref[at, 2 * width :] = raw[:, 2 * width :].astype(BF16)
    vt_ref[...] = jnp.transpose(qkv_ref[:, 2 * width :])
    for i in range(rows // block):
        here = slice(i * block, (i + 1) * block)
        reach = (i + 1) * block

        @pl.when(i * block < length)
        def _():
            query = qkv_ref[here, :width]
            keys = qkv_ref[:reach, width : 2 * width]
            keep = keep_mask(block, i * block, length)
            pieces = []
            for head in range(heads):
                masked = jnp.where(head_mask(query.shape, head), query, jnp.zeros_like(query))
                s_ref[:reach, :] = dot(keys, masked, 1, 1)
                s_ref[here, :] = jnp.where(keep, s_ref[here, :], NEG)
                scores = s_ref[:reach, :] * (SCALE * LOG2E)
                top = jnp.max(scores, axis=0, keepdims=True)
                weights = jnp.exp2(scores - top)
                total = jnp.sum(weights, axis=0, keepdims=True)
                low = weights.astype(BF16)
                mixed = dot(vt_ref[head * HD : (head + 1) * HD, :reach], low, 1, 0)
                pieces.append(mixed * (1.0 / total))
                lse_ref[head : head + 1, here] = top + jnp.log2(total)
            attn_ref[here, :] = jnp.transpose(jnp.concatenate(pieces, axis=0)).astype(BF16)

        @pl.when(i * block >= length)
        def _():
            attn_ref[here, :] = jnp.zeros((block, width), BF16)
            lse_ref[:, here] = jnp.zeros((lse_ref.shape[0], block), F32)

    for s, half in enumerate((attn_own_ref, attn_sib_ref)):
        for k in range(chips):
            at = pl.ds(piece_rows(where_ref, s, k, chips, size), size)
            half[k * size : (k + 1) * size, :] = attn_ref[at, :]


def backward_kernel(
    chips, heads, where_ref, own_ref, sib_ref, qkv_ref, lse_ref, cos_ref, plus_ref, minus_ref,
    grad_own_ref, grad_sib_ref, bias_grad_ref,
    g_ref, kt_ref, qs_ref, gs_ref, p_ref, d_ref, pcat_ref, scat_ref, dq_ref, dk_ref, dv_ref,
):
    width = heads * HD
    rows = qkv_ref.shape[0]
    size = rows // (2 * chips)
    block = min(256, rows)
    length = where_ref[2]
    for s, half in enumerate((own_ref, sib_ref)):
        for k in range(chips):
            at = pl.ds(piece_rows(where_ref, s, k, chips, size), size)
            g_ref[at, :] = half[k * size : (k + 1) * size, :]
    kt_ref[...] = jnp.transpose(qkv_ref[:, width : 2 * width])
    dk_ref[...] = jnp.zeros_like(dk_ref)
    dv_ref[...] = jnp.zeros_like(dv_ref)
    for i in range(rows // block):
        here = slice(i * block, (i + 1) * block)
        reach = (i + 1) * block

        @pl.when(i * block < length)
        def _():
            query = qkv_ref[here, :width]
            grad = g_ref[here, :]
            keys = qkv_ref[:reach, width : 2 * width]
            values = qkv_ref[:reach, 2 * width :]
            keep = keep_mask(block, i * block, length)
            pieces = []
            for head in range(heads):
                mask = head_mask(query.shape, head)
                cols = slice(head * block, (head + 1) * block)
                qs_ref[cols, :] = jnp.where(mask, query, jnp.zeros_like(query))
                gs_ref[cols, :] = jnp.where(mask, grad, jnp.zeros_like(grad))
                p_ref[:reach, :] = dot(keys, qs_ref[cols, :], 1, 1)
                p_ref[here, :] = jnp.where(keep, p_ref[here, :], NEG)
                weights = jnp.exp2(p_ref[:reach, :] * (SCALE * LOG2E) - lse_ref[head : head + 1, here])
                pcat_ref[:reach, cols] = weights.astype(BF16)
                p_ref[:reach, :] = weights
                d_ref[:reach, :] = dot(values, gs_ref[cols, :], 1, 1)
                offset = jnp.sum(p_ref[:reach, :] * d_ref[:reach, :], axis=0, keepdims=True)
                low = (p_ref[:reach, :] * (d_ref[:reach, :] - offset)).astype(BF16)
                scat_ref[:reach, cols] = low
                pieces.append(dot(kt_ref[head * HD : (head + 1) * HD, :reach], low, 1, 0))
            dv_ref[:reach, :] += dot(pcat_ref[:reach, :], gs_ref[...], 1, 0)
            dk_ref[:reach, :] += dot(scat_ref[:reach, :], qs_ref[...], 1, 0)
            dq_ref[here, :] = jnp.transpose(jnp.concatenate(pieces, axis=0))

        @pl.when(i * block >= length)
        def _():
            dq_ref[here, :] = jnp.zeros((block, width), F32)

    sums = [jnp.zeros((1, width), F32) for _ in range(3)]
    for s, half in enumerate((grad_own_ref, grad_sib_ref)):
        for k in range(chips):
            at = pl.ds(piece_rows(where_ref, s, k, chips, size), size)
            to = slice(k * size, (k + 1) * size)
            cos, plus, minus = cos_ref[at, :], plus_ref[at, :], minus_ref[at, :]
            parts = (
                turn(dq_ref[at, :] * SCALE, cos, -plus, -minus),
                turn(dk_ref[at, :] * SCALE, cos, -plus, -minus),
                dv_ref[at, :],
            )
            for j, part in enumerate(parts):
                low = part.astype(BF16)
                half[to, j * width : (j + 1) * width] = low
                sums[j] = sums[j] + jnp.sum(low.astype(F32), axis=0, keepdims=True)
    bias_grad_ref[...] = jnp.concatenate([jnp.broadcast_to(x, (8, width)) for x in sums], axis=1)


VMEM = pl.BlockSpec(memory_space=pltpu.VMEM)
SMEM = pl.BlockSpec(memory_space=pltpu.SMEM)


def attend(where, own, sib, bias, tables, chips, heads):
    width = heads * HD
    rows = 2 * own.shape[0]
    block = min(256, rows)
    return pl.pallas_call(
        functools.partial(forward_kernel, chips, heads),
        out_shape=(
            jax.ShapeDtypeStruct((rows // 2, width), BF16),
            jax.ShapeDtypeStruct((rows // 2, width), BF16),
            jax.ShapeDtypeStruct((rows, 3 * width), BF16),
            jax.ShapeDtypeStruct((8, rows), F32),
        ),
        in_specs=[SMEM] + [VMEM] * 6,
        out_specs=[VMEM] * 4,
        scratch_shapes=[
            pltpu.VMEM((width, rows), BF16),
            pltpu.VMEM((rows, block), F32),
            pltpu.VMEM((rows, width), BF16),
        ],
        compiler_params=pltpu.CompilerParams(vmem_limit_bytes=32 << 20),
        cost_estimate=pl.CostEstimate(
            flops=heads * rows * rows * 512, transcendentals=heads * rows * rows // 2, bytes_accessed=8 << 20
        ),
        name="attend",
    )(where, own, sib, bias, *tables)


def attend_back(where, own, sib, qkv, lse, tables, chips, heads):
    width = heads * HD
    rows = 2 * own.shape[0]
    block = min(256, rows)
    return pl.pallas_call(
        functools.partial(backward_kernel, chips, heads),
        out_shape=(
            jax.ShapeDtypeStruct((rows // 2, 3 * width), BF16),
            jax.ShapeDtypeStruct((rows // 2, 3 * width), BF16),
            jax.ShapeDtypeStruct((8, 3 * width), F32),
        ),
        in_specs=[SMEM] + [VMEM] * 7,
        out_specs=[VMEM] * 3,
        scratch_shapes=[
            pltpu.VMEM((rows, width), BF16),
            pltpu.VMEM((width, rows), BF16),
            pltpu.VMEM((heads * block, width), BF16),
            pltpu.VMEM((heads * block, width), BF16),
            pltpu.VMEM((rows, block), F32),
            pltpu.VMEM((rows, block), F32),
            pltpu.VMEM((rows, heads * block), BF16),
            pltpu.VMEM((rows, heads * block), BF16),
            pltpu.VMEM((rows, width), F32),
            pltpu.VMEM((rows, width), F32),
            pltpu.VMEM((rows, width), F32),
        ],
        compiler_params=pltpu.CompilerParams(vmem_limit_bytes=40 << 20),
        cost_estimate=pl.CostEstimate(
            flops=heads * rows * rows * 1280, transcendentals=heads * rows * rows // 2, bytes_accessed=8 << 20
        ),
        name="attend_back",
    )(where, own, sib, qkv, lse, *tables)


def rope_tables(rows, width):
    half = ROT // 2
    lane = jnp.arange(width, dtype=jnp.int32) % HD
    power = (lane % half).astype(F32)
    frequency = ROPE_BASE ** (-(2.0 * power) / ROT)
    angles = jnp.arange(rows, dtype=F32)[:, None] * frequency[None, :]
    cos = jnp.where(lane < ROT, jnp.cos(angles), 1.0)
    sine = jnp.sin(angles)
    plus = jnp.where((lane >= half) & (lane < ROT), sine, 0.0)
    minus = jnp.where(lane < half, -sine, 0.0)
    return (cos, plus, minus)


def local(
    tokens,
    out_grad,
    row_seq,
    seq_lengths,
    norm1_gain,
    norm1_bias,
    qkv_weight,
    qk_bias,
    v_bias,
    out_weight,
    norm2_gain,
    norm2_bias,
    gate_weight,
    up_weight,
    down_weight,
):
    line = Line()
    batches, seq_here, rows_here, depth = tokens.shape
    assert rows_here == 1
    chips = line.chips
    seq_full = seq_here * line.devices
    width = qkv_weight.shape[2]
    heads_here = width // HD
    piece = seq_here

    table = jnp.arange(seq_lengths.shape[0], dtype=jnp.int32)
    row_len = jnp.sum(jnp.where(row_seq[..., None] == table, seq_lengths, 0), axis=-1)[:, 0]
    positions = lax.axis_index("heads") * seq_here + jnp.arange(seq_here, dtype=jnp.int32)
    tables = rope_tables(seq_full, width)

    vectors = jnp.stack([norm1_gain, norm1_bias, norm2_gain, norm2_bias])
    vectors = small_gather(small_gather(small_gather(vectors, "heads", "core"), "heads", "chip"), "batch")
    gain_one, shift_one, gain_two, shift_two = (vectors[i] for i in range(4))

    qkv_flat = jnp.concatenate([qkv_weight[:, j] for j in range(3)], axis=1)
    bias = jnp.concatenate([qk_bias[0].reshape(-1), qk_bias[1].reshape(-1), v_bias.reshape(-1)])
    bias = bias.astype(F32)[None, :]
    gate_full = lax.all_gather(gate_weight, "batch", axis=0, tiled=True)
    up_full = lax.all_gather(up_weight, "batch", axis=0, tiled=True)
    down_full = lax.all_gather(down_weight, "batch", axis=0, tiled=True)

    def gather_halves(block):
        own = line.gather(block)
        return (own, line.swap(own))

    def scatter_halves(product):
        received = line.swap(product(1).astype(BF16))
        summed = (product(0) + received.astype(F32)).astype(BF16)
        line.token = summed
        return line.scatter([summed[k * piece : (k + 1) * piece] for k in range(chips)])

    class Row:
        pass

    rows = []
    for r in range(batches):
        row = Row()
        row.length = row_len[r]
        row.where = jnp.stack([line.chip, line.core, row.length]).astype(jnp.int32)
        row.valid = (positions < row.length).astype(F32)[:, None]
        row.grad_y = (out_grad[r, :, 0].astype(F32) * row.valid).astype(BF16)
        row.inputs = tokens[r, :, 0].astype(F32)
        normed, row.unit_one, row.inverse_one = row_norm(row.inputs, gain_one, shift_one)
        row.normed_one = normed.astype(BF16)
        rows.append(row)

    def stage_attend(row, *earlier):
        raw = [dot(after(x, *earlier), qkv_flat, 1, 0) for x in row.ones]
        *row.attn, row.qkv, row.lse = attend(row.where, *raw, bias, tables, chips, heads_here)
        row.branch = scatter_halves(lambda s: dot(row.attn[s], out_weight, 1, 0))
        return row.attn[0]

    def stage_norm(row, *earlier):
        row.state = row.inputs + after(row.branch, *earlier)
        normed, row.unit_two, row.inverse_two = row_norm(row.state, gain_two, shift_two)
        row.normed_two = normed.astype(BF16)
        row.twos = gather_halves(row.normed_two)
        return row.normed_two

    def stage_mlp(row, *earlier):
        row.inner, row.grad_gate, row.grad_up = [], [], []
        for s in range(2):
            twos = after(row.twos[s], *earlier)
            gate = dot(twos, gate_full, 1, 0)
            up = dot(twos, up_full, 1, 0)
            sigma = jax.nn.sigmoid(gate)
            silu = gate * sigma
            row.inner.append((silu * up).astype(BF16))
            grad_inner = dot(row.grads[s], down_full, 1, 0)
            row.grad_gate.append((grad_inner * up * sigma * (1.0 + gate * (1.0 - sigma))).astype(BF16))
            row.grad_up.append((grad_inner * silu).astype(BF16))
        row.grad_two = scatter_halves(
            lambda s: dot(row.grad_gate[s], gate_full, 1, 1) + dot(row.grad_up[s], up_full, 1, 1)
        )
        return row.grad_gate[0]

    def stage_state(row, *earlier):
        row.grad_two = after(row.grad_two, *earlier)
        row.grad_state = row.grad_y.astype(F32) + norm_back(
            row.grad_two, row.unit_two, row.inverse_two, gain_two
        )
        low = row.grad_state.astype(BF16)
        row.states = gather_halves(low)
        return low

    def stage_back(row, *earlier):
        grad_attn = [dot(after(x, *earlier), out_weight, 1, 1).astype(BF16) for x in row.states]
        *row.grad_qkv, bias_grad = attend_back(
            row.where, *grad_attn, row.qkv, row.lse, tables, chips, heads_here
        )
        row.bias_grad = bias_grad[0]
        row.grad_one = scatter_halves(lambda s: dot(row.grad_qkv[s], qkv_flat, 1, 1))
        return row.grad_qkv[0]

    def stage_down(row, *earlier):
        inner = line.spread([after(x, *earlier) for x in row.inner])
        low = dot(inner, down_full, 1, 1).astype(BF16)
        row.mlp = lax.psum_scatter(low, "heads", scatter_dimension=0, tiled=True).astype(F32)

    def stage_end(row):
        row.input_grad = row.grad_state + norm_back(
            row.grad_one, row.unit_one, row.inverse_one, gain_one
        )
        row.norms = jnp.stack(
            [
                jnp.sum(row.grad_one * row.unit_one, axis=0),
                jnp.sum(row.grad_one, axis=0),
                jnp.sum(row.grad_two * row.unit_two, axis=0),
                jnp.sum(row.grad_two, axis=0),
            ]
        )
        row.output = ((row.state + row.mlp) * row.valid).astype(BF16)

    first, second = rows
    for row in rows:
        row.ones = gather_halves(row.normed_one)
        row.grads = line.pick(lax.all_gather(row.grad_y, "heads", axis=0, tiled=True))
    token = stage_attend(first)
    token = stage_attend(second, token)
    token = stage_norm(first, token)
    token = stage_norm(second, token)
    token = stage_mlp(first, token)
    token = stage_mlp(second, token)
    middle = line.token
    stage_down(first, token)
    stage_down(second, token)
    token = stage_state(first, token)
    token = stage_state(second, token)
    token = stage_back(first, token)
    token = stage_back(second, token)
    last = line.token
    for row in rows:
        stage_end(row)

    parts = {}

    def weight_grad(left, right, dim, *earlier):
        total = None
        for row in rows:
            for s in range(2):
                term = dot(after(getattr(row, left)[s], *earlier), getattr(row, right)[s], 0, 0)
                total = term if total is None else total + term
        low = parts[left] = total.astype(BF16)
        return lax.psum_scatter(low, "batch", scatter_dimension=dim, tiled=True).astype(F32)

    down_grad = weight_grad("grads", "inner", 0, middle)
    gate_grad = weight_grad("twos", "grad_gate", 0, middle)
    up_grad = weight_grad("twos", "grad_up", 0, middle)
    out_grad_w = weight_grad("attn", "states", 1, last)
    qkv_grad = weight_grad("ones", "grad_qkv", 0, last)
    qkv_grad = jnp.stack([qkv_grad[:, j * width : (j + 1) * width] for j in range(3)], axis=1)

    bias_sum = functools.reduce(jnp.add, [row.bias_grad for row in rows])
    bias_sum = small_scatter(bias_sum.reshape(3 * heads_here, HD), "batch", 1)
    bias_sum = bias_sum.reshape(3, heads_here, -1)
    norm_sum = functools.reduce(jnp.add, [row.norms for row in rows])
    norm_sum = small_scatter(small_scatter(small_scatter(norm_sum, "batch", 1), "heads", 1, "chip"), "heads", 1, "core")
    return (
        jnp.stack([row.output for row in rows])[:, :, None],
        jnp.stack([row.input_grad.astype(BF16) for row in rows])[:, :, None],
        norm_sum[0],
        norm_sum[1],
        qkv_grad,
        bias_sum[:2],
        bias_sum[2],
        out_grad_w,
        norm_sum[2],
        norm_sum[3],
        gate_grad,
        up_grad,
        down_grad,
    )


def solution(mesh):
    placed = (
        P(None, "heads", "batch", None),
        P(None, "heads", "batch", None),
        P(None, "batch"),
        P(),
        P(("batch", "heads")),
        P(("batch", "heads")),
        P(None, None, "heads"),
        P(None, "heads", None),
        P("heads", None),
        P("heads", None),
        P(("batch", "heads")),
        P(("batch", "heads")),
        P("batch", "heads"),
        P("batch", "heads"),
        P("batch", "heads"),
    )
    return jax.shard_map(
        local,
        mesh=mesh,
        in_specs=placed,
        out_specs=(
            P(None, "heads", "batch", None),
            P(None, "heads", "batch", None),
            P(("batch", "heads")),
            P(("batch", "heads")),
            P("batch", None, "heads"),
            P(None, "heads", "batch"),
            P("heads", "batch"),
            P("heads", "batch"),
            P(("batch", "heads")),
            P(("batch", "heads")),
            P("batch", "heads"),
            P("batch", "heads"),
            P("batch", "heads"),
        ),
        check_vma=False,
    )
```

```python
import functools
import math

import jax
import jax.numpy as jnp
from jax import lax
from jax.experimental import pallas as pl
from jax.experimental.pallas import tpu as pltpu
from jax.sharding import PartitionSpec as P

HD = 64
ROT = 16
EPS = 1e-05
NEG = -1e30
ROPE_BASE = 10000.0
SCALE = HD ** (-0.5)
LOG2E = math.log2(math.e)
F32 = jnp.float32
BF16 = jnp.bfloat16


def dot(a, b, ca, cb):
    return lax.dot_general(a, b, (((ca,), (cb,)), ((), ())), preferred_element_type=F32)


def row_norm(values, gain_vec, shift_vec):
    average = jnp.mean(values, axis=-1, keepdims=True)
    centred = values - average
    inverse = lax.rsqrt(jnp.mean(centred * centred, axis=-1, keepdims=True) + EPS)
    unit_rows = centred * inverse
    return (unit_rows * gain_vec + shift_vec, unit_rows, inverse)


def norm_back(gradient, unit_rows, inverse, gain_vec):
    scaled_grad = gradient * gain_vec
    return inverse * (
        scaled_grad
        - jnp.mean(scaled_grad, axis=-1, keepdims=True)
        - unit_rows * jnp.mean(scaled_grad * unit_rows, axis=-1, keepdims=True)
    )


class Line:
    def __init__(self):
        self.devices = lax.axis_size("heads")
        self.chips = self.devices // 2
        index = lax.axis_index("heads")
        self.chip = index // 2
        self.core = index % 2

    def hop(self, value, sources, step):
        pairs = [(2 * i + c, 2 * (i + step) + c) for i in sources for c in range(2)]
        return lax.ppermute(value, "heads", pairs)

    def swap(self, value):
        pairs = [(2 * i + c, 2 * i + 1 - c) for i in range(self.chips) for c in range(2)]
        return lax.ppermute(value, "heads", pairs)

    def place(self, k, core):
        return 2 * ((self.chip - k) % self.chips) + core

    def pick(self, full):
        size = full.shape[0] // self.devices
        return tuple(
            jnp.concatenate(
                [lax.dynamic_slice_in_dim(full, self.place(k, core) * size, size, 0) for k in range(self.chips)]
            )
            for core in (self.core, 1 - self.core)
        )

    def spread(self, halves):
        size = halves[0].shape[0] // self.chips
        full = jnp.zeros((size * self.devices, halves[0].shape[1]), halves[0].dtype)
        for half, core in zip(halves, (self.core, 1 - self.core)):
            for k in range(self.chips):
                rows = half[k * size : (k + 1) * size]
                full = lax.dynamic_update_slice_in_dim(full, rows, self.place(k, core) * size, 0)
        return full

    def gather(self, block):
        n = self.chips
        ups, downs = [block], [block]
        for step in range(1, n):
            ups.append(self.hop(ups[-1], range(step - 1, n - 1), 1))
            downs.append(self.hop(downs[-1], range(1, n - step + 1), -1))
        pieces = [block]
        for k in range(1, n):
            pieces.append(jnp.where(self.chip >= k, ups[k], downs[n - k]))
        return jnp.concatenate(pieces, axis=0)

    def scatter(self, pieces):
        n = self.chips
        up = down = None
        for m in range(n - 1, 0, -1):
            value_up = pieces[n - m] if up is None else add_low(pieces[n - m], up)
            value_down = pieces[m] if down is None else add_low(pieces[m], down)
            up = self.hop(value_up, range(0, n - m), 1)
            down = self.hop(value_down, range(m, n), -1)
        return pieces[0].astype(F32) + up.astype(F32) + down.astype(F32)


def after(value, *earlier):
    return lax.optimization_barrier((value, *earlier))[0]


def add_low(a, b):
    return (a.astype(F32) + b.astype(F32)).astype(BF16)


def ring(axis, group):
    size, index = lax.axis_size(axis), lax.axis_index(axis)
    if group == "core":
        return 2, index % 2, lambda k: [(i, i ^ k) for i in range(size)]
    if group == "chip":
        return size // 2, index // 2, lambda k: [(i, (i + 2 * k) % size) for i in range(size)]
    return size, index, lambda k: [(i, (i + k) % size) for i in range(size)]


def shifts(value_of, axis, group):
    n, _, pairs = ring(axis, group)
    return [value_of(0)] + [lax.ppermute(value_of(k), axis, pairs(k)) for k in range(1, n)]


def small_gather(value, axis, group="all"):
    n, me, _ = ring(axis, group)
    received = shifts(lambda k: value, axis, group)
    width = value.shape[1]
    ordered = jnp.concatenate(received[::-1], axis=1)
    doubled = jnp.concatenate([ordered, ordered], axis=1)
    return lax.dynamic_slice_in_dim(doubled, (n - 1 - me) * width, n * width, 1)


def small_scatter(value, axis, dim, group="all"):
    n, me, _ = ring(axis, group)
    width = value.shape[dim] // n

    def part(k):
        return lax.dynamic_slice_in_dim(value, ((me + k) % n) * width, width, dim)

    return functools.reduce(jnp.add, shifts(part, axis, group))


def piece_rows(where_ref, s, k, chips, size):
    chip, core = where_ref[0], where_ref[1]
    owner = lax.rem(chip - k + chips, chips)
    other = core if s == 0 else 1 - core
    return pl.multiple_of((2 * owner + other) * size, size)


def head_mask(shape, head):
    lane = lax.broadcasted_iota(jnp.int32, shape, len(shape) - 1)
    return (lane >= head * HD) & (lane < (head + 1) * HD)


def keep_mask(size, start, length):
    key = lax.broadcasted_iota(jnp.int32, (size, size), 0)
    query = lax.broadcasted_iota(jnp.int32, (size, size), 1)
    return (key <= query) & (key + start < length)


def turn(x, cos, plus, minus):
    half = ROT // 2
    width = x.shape[1]
    return x * cos + pltpu.roll(x, half, 1) * plus + pltpu.roll(x, width - half, 1) * minus


def forward_kernel(
    chips, heads, where_ref, own_ref, sib_ref, bias_ref, cos_ref, plus_ref, minus_ref,
    attn_own_ref, attn_sib_ref, qkv_ref, lse_ref, vt_ref, s_ref, attn_ref,
):
    width = heads * HD
    rows = qkv_ref.shape[0]
    size = rows // (2 * chips)
    block = min(256, rows)
    length = where_ref[2]
    for s, half in enumerate((own_ref, sib_ref)):
        for k in range(chips):
            at = pl.ds(piece_rows(where_ref, s, k, chips, size), size)
            raw = half[k * size : (k + 1) * size, :] + bias_ref[...]
            cos, plus, minus = cos_ref[at, :], plus_ref[at, :], minus_ref[at, :]
            for part in range(2):
                x = raw[:, part * width : (part + 1) * width]
                qkv_ref[at, part * width : (part + 1) * width] = turn(x, cos, plus, minus).astype(BF16)
            qkv_ref[at, 2 * width :] = raw[:, 2 * width :].astype(BF16)
    vt_ref[...] = jnp.transpose(qkv_ref[:, 2 * width :])
    for i in range(rows // block):
        here = slice(i * block, (i + 1) * block)
        reach = (i + 1) * block

        @pl.when(i * block < length)
        def _():
            query = qkv_ref[here, :width]
            keys = qkv_ref[:reach, width : 2 * width]
            keep = keep_mask(block, i * block, length)
            pieces = []
            for head in range(heads):
                masked = jnp.where(head_mask(query.shape, head), query, jnp.zeros_like(query))
                s_ref[:reach, :] = dot(keys, masked, 1, 1)
                s_ref[here, :] = jnp.where(keep, s_ref[here, :], NEG)
                scores = s_ref[:reach, :] * (SCALE * LOG2E)
                top = jnp.max(scores, axis=0, keepdims=True)
                weights = jnp.exp2(scores - top)
                total = jnp.sum(weights, axis=0, keepdims=True)
                low = weights.astype(BF16)
                mixed = dot(vt_ref[head * HD : (head + 1) * HD, :reach], low, 1, 0)
                pieces.append(mixed * (1.0 / total))
                lse_ref[head : head + 1, here] = top + jnp.log2(total)
            attn_ref[here, :] = jnp.transpose(jnp.concatenate(pieces, axis=0)).astype(BF16)

        @pl.when(i * block >= length)
        def _():
            attn_ref[here, :] = jnp.zeros((block, width), BF16)
            lse_ref[:, here] = jnp.zeros((lse_ref.shape[0], block), F32)

    for s, half in enumerate((attn_own_ref, attn_sib_ref)):
        for k in range(chips):
            at = pl.ds(piece_rows(where_ref, s, k, chips, size), size)
            half[k * size : (k + 1) * size, :] = attn_ref[at, :]


def backward_kernel(
    chips, heads, where_ref, own_ref, sib_ref, qkv_ref, lse_ref, cos_ref, plus_ref, minus_ref,
    grad_own_ref, grad_sib_ref, bias_grad_ref,
    g_ref, kt_ref, qs_ref, gs_ref, p_ref, d_ref, pcat_ref, scat_ref, dq_ref, dk_ref, dv_ref,
):
    width = heads * HD
    rows = qkv_ref.shape[0]
    size = rows // (2 * chips)
    block = min(256, rows)
    length = where_ref[2]
    for s, half in enumerate((own_ref, sib_ref)):
        for k in range(chips):
            at = pl.ds(piece_rows(where_ref, s, k, chips, size), size)
            g_ref[at, :] = half[k * size : (k + 1) * size, :]
    kt_ref[...] = jnp.transpose(qkv_ref[:, width : 2 * width])
    dk_ref[...] = jnp.zeros_like(dk_ref)
    dv_ref[...] = jnp.zeros_like(dv_ref)
    for i in range(rows // block):
        here = slice(i * block, (i + 1) * block)
        reach = (i + 1) * block

        @pl.when(i * block < length)
        def _():
            query = qkv_ref[here, :width]
            grad = g_ref[here, :]
            keys = qkv_ref[:reach, width : 2 * width]
            values = qkv_ref[:reach, 2 * width :]
            keep = keep_mask(block, i * block, length)
            pieces = []
            for head in range(heads):
                mask = head_mask(query.shape, head)
                cols = slice(head * block, (head + 1) * block)
                qs_ref[cols, :] = jnp.where(mask, query, jnp.zeros_like(query))
                gs_ref[cols, :] = jnp.where(mask, grad, jnp.zeros_like(grad))
                p_ref[:reach, :] = dot(keys, qs_ref[cols, :], 1, 1)
                p_ref[here, :] = jnp.where(keep, p_ref[here, :], NEG)
                weights = jnp.exp2(p_ref[:reach, :] * (SCALE * LOG2E) - lse_ref[head : head + 1, here])
                pcat_ref[:reach, cols] = weights.astype(BF16)
                p_ref[:reach, :] = weights
                d_ref[:reach, :] = dot(values, gs_ref[cols, :], 1, 1)
                offset = jnp.sum(p_ref[:reach, :] * d_ref[:reach, :], axis=0, keepdims=True)
                low = (p_ref[:reach, :] * (d_ref[:reach, :] - offset)).astype(BF16)
                scat_ref[:reach, cols] = low
                pieces.append(dot(kt_ref[head * HD : (head + 1) * HD, :reach], low, 1, 0))
            dv_ref[:reach, :] += dot(pcat_ref[:reach, :], gs_ref[...], 1, 0)
            dk_ref[:reach, :] += dot(scat_ref[:reach, :], qs_ref[...], 1, 0)
            dq_ref[here, :] = jnp.transpose(jnp.concatenate(pieces, axis=0))

        @pl.when(i * block >= length)
        def _():
            dq_ref[here, :] = jnp.zeros((block, width), F32)

    sums = [jnp.zeros((1, width), F32) for _ in range(3)]
    for s, half in enumerate((grad_own_ref, grad_sib_ref)):
        for k in range(chips):
            at = pl.ds(piece_rows(where_ref, s, k, chips, size), size)
            to = slice(k * size, (k + 1) * size)
            cos, plus, minus = cos_ref[at, :], plus_ref[at, :], minus_ref[at, :]
            parts = (
                turn(dq_ref[at, :] * SCALE, cos, -plus, -minus),
                turn(dk_ref[at, :] * SCALE, cos, -plus, -minus),
                dv_ref[at, :],
            )
            for j, part in enumerate(parts):
                low = part.astype(BF16)
                half[to, j * width : (j + 1) * width] = low
                sums[j] = sums[j] + jnp.sum(low.astype(F32), axis=0, keepdims=True)
    bias_grad_ref[...] = jnp.concatenate([jnp.broadcast_to(x, (8, width)) for x in sums], axis=1)


VMEM = pl.BlockSpec(memory_space=pltpu.VMEM)
SMEM = pl.BlockSpec(memory_space=pltpu.SMEM)


def attend(where, own, sib, bias, tables, chips, heads):
    width = heads * HD
    rows = 2 * own.shape[0]
    block = min(256, rows)
    return pl.pallas_call(
        functools.partial(forward_kernel, chips, heads),
        out_shape=(
            jax.ShapeDtypeStruct((rows // 2, width), BF16),
            jax.ShapeDtypeStruct((rows // 2, width), BF16),
            jax.ShapeDtypeStruct((rows, 3 * width), BF16),
            jax.ShapeDtypeStruct((8, rows), F32),
        ),
        in_specs=[SMEM] + [VMEM] * 6,
        out_specs=[VMEM] * 4,
        scratch_shapes=[
            pltpu.VMEM((width, rows), BF16),
            pltpu.VMEM((rows, block), F32),
            pltpu.VMEM((rows, width), BF16),
        ],
        compiler_params=pltpu.CompilerParams(vmem_limit_bytes=32 << 20),
        cost_estimate=pl.CostEstimate(
            flops=heads * rows * rows * 512, transcendentals=heads * rows * rows // 2, bytes_accessed=8 << 20
        ),
        name="attend",
    )(where, own, sib, bias, *tables)


def attend_back(where, own, sib, qkv, lse, tables, chips, heads):
    width = heads * HD
    rows = 2 * own.shape[0]
    block = min(256, rows)
    return pl.pallas_call(
        functools.partial(backward_kernel, chips, heads),
        out_shape=(
            jax.ShapeDtypeStruct((rows // 2, 3 * width), BF16),
            jax.ShapeDtypeStruct((rows // 2, 3 * width), BF16),
            jax.ShapeDtypeStruct((8, 3 * width), F32),
        ),
        in_specs=[SMEM] + [VMEM] * 7,
        out_specs=[VMEM] * 3,
        scratch_shapes=[
            pltpu.VMEM((rows, width), BF16),
            pltpu.VMEM((width, rows), BF16),
            pltpu.VMEM((heads * block, width), BF16),
            pltpu.VMEM((heads * block, width), BF16),
            pltpu.VMEM((rows, block), F32),
            pltpu.VMEM((rows, block), F32),
            pltpu.VMEM((rows, heads * block), BF16),
            pltpu.VMEM((rows, heads * block), BF16),
            pltpu.VMEM((rows, width), F32),
            pltpu.VMEM((rows, width), F32),
            pltpu.VMEM((rows, width), F32),
        ],
        compiler_params=pltpu.CompilerParams(vmem_limit_bytes=40 << 20),
        cost_estimate=pl.CostEstimate(
            flops=heads * rows * rows * 1280, transcendentals=heads * rows * rows // 2, bytes_accessed=8 << 20
        ),
        name="attend_back",
    )(where, own, sib, qkv, lse, *tables)


def rope_tables(rows, width):
    half = ROT // 2
    lane = jnp.arange(width, dtype=jnp.int32) % HD
    power = (lane % half).astype(F32)
    frequency = ROPE_BASE ** (-(2.0 * power) / ROT)
    angles = jnp.arange(rows, dtype=F32)[:, None] * frequency[None, :]
    cos = jnp.where(lane < ROT, jnp.cos(angles), 1.0)
    sine = jnp.sin(angles)
    plus = jnp.where((lane >= half) & (lane < ROT), sine, 0.0)
    minus = jnp.where(lane < half, -sine, 0.0)
    return (cos, plus, minus)


def local(
    tokens,
    out_grad,
    row_seq,
    seq_lengths,
    norm1_gain,
    norm1_bias,
    qkv_weight,
    qk_bias,
    v_bias,
    out_weight,
    norm2_gain,
    norm2_bias,
    gate_weight,
    up_weight,
    down_weight,
):
    line = Line()
    batches, seq_here, rows_here, depth = tokens.shape
    assert rows_here == 1
    chips = line.chips
    seq_full = seq_here * line.devices
    width = qkv_weight.shape[2]
    heads_here = width // HD
    piece = seq_here

    table = jnp.arange(seq_lengths.shape[0], dtype=jnp.int32)
    row_len = jnp.sum(jnp.where(row_seq[..., None] == table, seq_lengths, 0), axis=-1)[:, 0]
    positions = lax.axis_index("heads") * seq_here + jnp.arange(seq_here, dtype=jnp.int32)
    tables = rope_tables(seq_full, width)

    vectors = jnp.stack([norm1_gain, norm1_bias, norm2_gain, norm2_bias])
    vectors = small_gather(small_gather(small_gather(vectors, "heads", "core"), "heads", "chip"), "batch")
    gain_one, shift_one, gain_two, shift_two = (vectors[i] for i in range(4))

    qkv_flat = jnp.concatenate([qkv_weight[:, j] for j in range(3)], axis=1)
    bias = jnp.concatenate([qk_bias[0].reshape(-1), qk_bias[1].reshape(-1), v_bias.reshape(-1)])
    bias = bias.astype(F32)[None, :]
    gate_full = lax.all_gather(gate_weight, "batch", axis=0, tiled=True)
    up_full = lax.all_gather(up_weight, "batch", axis=0, tiled=True)
    down_full = lax.all_gather(down_weight, "batch", axis=0, tiled=True)

    def gather_halves(block):
        own = line.gather(block)
        return (own, line.swap(own))

    def scatter_halves(product):
        received = line.swap(product(1).astype(BF16))
        summed = (product(0) + received.astype(F32)).astype(BF16)
        line.token = summed
        return line.scatter([summed[k * piece : (k + 1) * piece] for k in range(chips)])

    class Row:
        pass

    rows = []
    for r in range(batches):
        row = Row()
        row.length = row_len[r]
        row.where = jnp.stack([line.chip, line.core, row.length]).astype(jnp.int32)
        row.valid = (positions < row.length).astype(F32)[:, None]
        row.grad_y = (out_grad[r, :, 0].astype(F32) * row.valid).astype(BF16)
        row.inputs = tokens[r, :, 0].astype(F32)
        normed, row.unit_one, row.inverse_one = row_norm(row.inputs, gain_one, shift_one)
        row.normed_one = normed.astype(BF16)
        rows.append(row)

    def stage_attend(row, *earlier):
        raw = [dot(after(x, *earlier), qkv_flat, 1, 0) for x in row.ones]
        *row.attn, row.qkv, row.lse = attend(row.where, *raw, bias, tables, chips, heads_here)
        row.branch = scatter_halves(lambda s: dot(row.attn[s], out_weight, 1, 0))
        return row.attn[0]

    def stage_norm(row, *earlier):
        row.state = row.inputs + after(row.branch, *earlier)
        normed, row.unit_two, row.inverse_two = row_norm(row.state, gain_two, shift_two)
        row.normed_two = normed.astype(BF16)
        row.twos = gather_halves(row.normed_two)
        return row.normed_two

    def stage_mlp(row, *earlier):
        row.inner, row.grad_gate, row.grad_up = [], [], []
        for s in range(2):
            twos = after(row.twos[s], *earlier)
            gate = dot(twos, gate_full, 1, 0)
            up = dot(twos, up_full, 1, 0)
            sigma = jax.nn.sigmoid(gate)
            silu = gate * sigma
            row.inner.append((silu * up).astype(BF16))
            grad_inner = dot(row.grads[s], down_full, 1, 0)
            row.grad_gate.append((grad_inner * up * sigma * (1.0 + gate * (1.0 - sigma))).astype(BF16))
            row.grad_up.append((grad_inner * silu).astype(BF16))
        row.grad_two = scatter_halves(
            lambda s: dot(row.grad_gate[s], gate_full, 1, 1) + dot(row.grad_up[s], up_full, 1, 1)
        )
        return row.grad_gate[0]

    def stage_state(row, *earlier):
        row.grad_two = after(row.grad_two, *earlier)
        row.grad_state = row.grad_y.astype(F32) + norm_back(
            row.grad_two, row.unit_two, row.inverse_two, gain_two
        )
        low = row.grad_state.astype(BF16)
        row.states = gather_halves(low)
        return low

    def stage_back(row, *earlier):
        grad_attn = [dot(after(x, *earlier), out_weight, 1, 1).astype(BF16) for x in row.states]
        *row.grad_qkv, bias_grad = attend_back(
            row.where, *grad_attn, row.qkv, row.lse, tables, chips, heads_here
        )
        row.bias_grad = bias_grad[0]
        row.grad_one = scatter_halves(lambda s: dot(row.grad_qkv[s], qkv_flat, 1, 1))
        return row.grad_qkv[0]

    def stage_down(row, *earlier):
        inner = line.spread([after(x, *earlier) for x in row.inner])
        low = dot(inner, down_full, 1, 1).astype(BF16)
        row.mlp = lax.psum_scatter(low, "heads", scatter_dimension=0, tiled=True).astype(F32)

    def stage_end(row):
        row.input_grad = row.grad_state + norm_back(
            row.grad_one, row.unit_one, row.inverse_one, gain_one
        )
        row.norms = jnp.stack(
            [
                jnp.sum(row.grad_one * row.unit_one, axis=0),
                jnp.sum(row.grad_one, axis=0),
                jnp.sum(row.grad_two * row.unit_two, axis=0),
                jnp.sum(row.grad_two, axis=0),
            ]
        )
        row.output = ((row.state + row.mlp) * row.valid).astype(BF16)

    first, second = rows
    for row in rows:
        row.ones = gather_halves(row.normed_one)
        row.grads = line.pick(lax.all_gather(row.grad_y, "heads", axis=0, tiled=True))
    token = stage_attend(first)
    token = stage_attend(second, token)
    token = stage_norm(first, token)
    token = stage_norm(second, token)
    token = stage_mlp(first, token)
    token = stage_mlp(second, token)
    middle = line.token
    stage_down(first, token)
    stage_down(second, token)
    token = stage_state(first)
    token = stage_state(second, token)
    token = stage_back(first, token)
    token = stage_back(second, token)
    last = line.token
    for row in rows:
        stage_end(row)

    parts = {}

    def weight_grad(left, right, dim, *earlier):
        total = None
        for row in rows:
            for s in range(2):
                term = dot(after(getattr(row, left)[s], *earlier), getattr(row, right)[s], 0, 0)
                total = term if total is None else total + term
        low = parts[left] = total.astype(BF16)
        return lax.psum_scatter(low, "batch", scatter_dimension=dim, tiled=True).astype(F32)

    down_grad = weight_grad("grads", "inner", 0, middle)
    gate_grad = weight_grad("twos", "grad_gate", 0, middle)
    up_grad = weight_grad("twos", "grad_up", 0, middle)
    out_grad_w = weight_grad("attn", "states", 1, last)
    qkv_grad = weight_grad("ones", "grad_qkv", 0, last)
    qkv_grad = jnp.stack([qkv_grad[:, j * width : (j + 1) * width] for j in range(3)], axis=1)

    bias_sum = functools.reduce(jnp.add, [row.bias_grad for row in rows])
    bias_sum = small_scatter(bias_sum.reshape(3 * heads_here, HD), "batch", 1)
    bias_sum = bias_sum.reshape(3, heads_here, -1)
    norm_sum = functools.reduce(jnp.add, [row.norms for row in rows])
    norm_sum = small_scatter(small_scatter(small_scatter(norm_sum, "batch", 1), "heads", 1, "chip"), "heads", 1, "core")
    return (
        jnp.stack([row.output for row in rows])[:, :, None],
        jnp.stack([row.input_grad.astype(BF16) for row in rows])[:, :, None],
        norm_sum[0],
        norm_sum[1],
        qkv_grad,
        bias_sum[:2],
        bias_sum[2],
        out_grad_w,
        norm_sum[2],
        norm_sum[3],
        gate_grad,
        up_grad,
        down_grad,
    )


def solution(mesh):
    placed = (
        P(None, "heads", "batch", None),
        P(None, "heads", "batch", None),
        P(None, "batch"),
        P(),
        P(("batch", "heads")),
        P(("batch", "heads")),
        P(None, None, "heads"),
        P(None, "heads", None),
        P("heads", None),
        P("heads", None),
        P(("batch", "heads")),
        P(("batch", "heads")),
        P("batch", "heads"),
        P("batch", "heads"),
        P("batch", "heads"),
    )
    return jax.shard_map(
        local,
        mesh=mesh,
        in_specs=placed,
        out_specs=(
            P(None, "heads", "batch", None),
            P(None, "heads", "batch", None),
            P(("batch", "heads")),
            P(("batch", "heads")),
            P("batch", None, "heads"),
            P(None, "heads", "batch"),
            P("heads", "batch"),
            P("heads", "batch"),
            P(("batch", "heads")),
            P(("batch", "heads")),
            P("batch", "heads"),
            P("batch", "heads"),
            P("batch", "heads"),
        ),
        check_vma=False,
    )
```
